32 devices in a mesh: branch: 2 (over x), tensor: 4 (over y, core), dp: 4 (over z).
Axes of the slice: x: 2, y: 2, z: 4, core: 2. Of those that a mesh axis runs over, the one named last changes fastest.
Arguments:
- tokens: bfloat16 [8192, 2048], P('dp'), may hold values from -6 to 6
- lengths: int32 [4], P('dp'), may hold values from 128 to 2048, as said below
- valid_mask: int32 [8192], P('dp'), may hold values 0 or 1
- ln1_gain: float32 [2048], replicated, may hold values from 0.1 to 1.9
- ln1_bias: float32 [2048], replicated, may hold values from -4 to 4
- qkv_weight: bfloat16 [2048, 6144], P('dp', 'tensor'), may hold values from -0.125 to 0.125
- qkv_bias: float32 [6144], P('tensor'), may hold values from -6 to 6
- out_weight: bfloat16 [2048, 2048], P('tensor', 'dp'), may hold values from -1 to 1
- out_bias: float32 [2048], replicated, may hold values from -4 to 4
- ln2_gain: float32 [2048], replicated, may hold values from 0.1 to 1.9
- ln2_bias: float32 [2048], replicated, may hold values from -4 to 4
- up_weight: bfloat16 [2048, 8192], P('dp', 'tensor'), may hold values from -0.125 to 0.125
- up_bias: float32 [8192], P('tensor'), may hold values from -6 to 6
- down_weight: bfloat16 [8192, 2048], P('tensor', 'dp'), may hold values from -0.0625 to 0.0625
- down_bias: float32 [2048], replicated, may hold values from -4 to 4
- out_grad: bfloat16 [8192, 2048], P('dp'), may hold values from -6 to 6
Outputs:
- layer_output: bfloat16 [8192, 2048], P('dp')
- x_grad: bfloat16 [8192, 2048], P('dp')
- ln1_gain_grad: float32 [2048], replicated
- ln1_bias_grad: float32 [2048], replicated
- qkv_weight_grad: float32 [2048, 6144], P(('branch', 'dp'), 'tensor')
- qkv_bias_grad: float32 [6144], P('tensor')
- out_weight_grad: float32 [2048, 2048], P('tensor', ('branch', 'dp'))
- out_bias_grad: float32 [2048], replicated
- ln2_gain_grad: float32 [2048], replicated
- ln2_bias_grad: float32 [2048], replicated
- up_weight_grad: float32 [2048, 8192], P(('branch', 'dp'), 'tensor')
- up_bias_grad: float32 [8192], P('tensor')
- down_weight_grad: float32 [8192, 2048], P('tensor', ('branch', 'dp'))
- down_bias_grad: float32 [2048], replicated
The draws below stay inside these ranges and needn't reach their ends.
Inputs may be any that keep to these rules, and one draw needn't show every extreme that they name: `lengths`: each sequence's length; the longest is exactly 2048. `valid_mask`: 1 marks a token that takes part; slots at or past their sequence's length are padding whatever the mask says.
All inputs are finite; a program needn't handle non-finite values. No bound on the sum of `valid_mask` on one device may be relied on, other than what follows from the above.
Results may differ from the reference program's by a relative error of at most 0.0098.
Values may be sent and summed in bfloat16 or wider, within the bound.
No kernel may reach another device: no remote copies, remote signals or barrier semaphores. Data moves between devices by JAX's collectives and lax.ppermute only.
A program may use at most 384 MiB of HBM per device.

```python
import jax
import jax.numpy as jnp
from jax import lax

D = 2048
HEADS = 8
HEAD_DIM = 256
FF = 8192
SEQ_LEN = 2048
MIN_LEN = 128
ROT = 64
NSEQ = 4
TOKENS = 8192


def draw_lengths(key, part):
    key_len, key_pick = jax.random.split(jax.random.fold_in(key, 11))
    drawn = jax.random.randint(key_len, (NSEQ,), MIN_LEN, SEQ_LEN + 1)
    chosen = jax.random.randint(key_pick, (), 0, NSEQ)
    return jnp.where(jnp.arange(NSEQ) == chosen, SEQ_LEN, drawn).astype(jnp.int32)


def touch_ends(array, key, least, top_value):
    longest = array.shape.index(max(array.shape))
    spots = []
    for shift in (0, 1):
        where = [jax.random.randint(jax.random.fold_in(key, axis), (), 0, length) for axis, length in enumerate(array.shape)]
        where[longest] = (where[longest] + shift) % array.shape[longest]
        spots.append(tuple(where))
    return array.at[spots[0]].set(least).at[spots[1]].set(top_value)


def levels(rng, extent, shards, low, high):
    level = 1.0
    for axis_at, shards_of in shards:
        steps = jax.random.uniform(jax.random.fold_in(jax.random.fold_in(rng, 6), axis_at), (shards_of,), jnp.float32, low / len(shards), high / len(shards))
        level = level * jnp.repeat(jnp.exp(steps), extent[axis_at] // shards_of).reshape((-1,) + (1,) * (len(extent) - 1 - axis_at))
    return level


def gaussian(rng, extent, spread, bound, pieces=(), held_as=jnp.bfloat16):
    level = levels(rng, extent, pieces, -0.22, 0.18) if pieces else 1.0
    values = jax.random.normal(rng, extent, jnp.float32) * spread * level
    return jnp.minimum(jnp.maximum(values, -bound), bound).astype(held_as)


def setup_inputs(seed: int = 0) -> dict:
    key_list = jax.random.split(jax.random.key(seed), 17)
    return {
        "tokens": gaussian(key_list[0], (TOKENS, D), 1.0, 6.0, ((0, 4),)),
        "lengths": draw_lengths(jax.random.fold_in(key_list[16], 71), 0),
        "valid_mask": touch_ends((jax.random.randint(key_list[2], (TOKENS,), 0, 8) < 7).astype(jnp.int32), jax.random.fold_in(key_list[2], 1), 0, 1),
        "ln1_gain": jnp.clip(1.0 + 0.18 * jax.random.normal(key_list[3], (D,), jnp.float32), 0.1, 1.9),
        "ln1_bias": gaussian(key_list[4], (D,), 0.3, 4.0, (), jnp.float32),
        "qkv_weight": gaussian(key_list[5], (D, 3 * D), D ** -0.5, 0.125, ((0, 4), (1, 4))),
        "qkv_bias": gaussian(key_list[6], (3 * D,), 0.5, 6.0, ((0, 4),), jnp.float32),
        "out_weight": gaussian(key_list[7], (D, D), (max(D // 64, 1)) ** -0.5, 1.0, ((0, 4), (1, 4))),
        "out_bias": gaussian(key_list[8], (D,), 0.3, 4.0, (), jnp.float32),
        "ln2_gain": jnp.clip(1.0 + 0.18 * jax.random.normal(key_list[9], (D,), jnp.float32), 0.1, 1.9),
        "ln2_bias": gaussian(key_list[10], (D,), 0.3, 4.0, (), jnp.float32),
        "up_weight": gaussian(key_list[11], (D, FF), D ** -0.5, 0.125, ((0, 4), (1, 4))),
        "up_bias": gaussian(key_list[12], (FF,), 0.5, 6.0, ((0, 4),), jnp.float32),
        "down_weight": gaussian(key_list[13], (FF, D), FF ** -0.5, 0.0625, ((0, 4), (1, 4))),
        "down_bias": gaussian(key_list[14], (D,), 0.3, 4.0, (), jnp.float32),
        "out_grad": gaussian(key_list[15], (TOKENS, D), 1.0, 6.0, ((0, 4),)),
    }


norm_eps = 1e-05
rope_base = 10000.0
masked_score = -1e+30
highest = lax.Precision.HIGHEST

@jax.custom_vjp
def low(v):
    return lax.optimization_barrier(v.astype(jnp.bfloat16)).astype(jnp.float32)

@jax.custom_vjp
def low_back(v):
    return v

def low_keep(v):
    return (low(v), None)

def low_pass(kept, grad):
    return (grad,)

def back_keep(v):
    return (v, None)

def back_low(kept, grad):
    return (low(grad),)
low.defvjp(low_keep, low_pass)
low_back.defvjp(back_keep, back_low)

def layer_norm(rows, gain, shift):
    row_mean = lax.optimization_barrier(jnp.mean(rows, axis=-1, keepdims=True))
    centred = rows - row_mean
    inv_std = lax.rsqrt(lax.optimization_barrier(jnp.mean(centred * centred, axis=-1, keepdims=True)) + norm_eps)
    return centred * inv_std * gain + shift

def rope_tables(length, rotary):
    half_rot = rotary // 2
    inv_freq = rope_base ** (-2.0 * jnp.arange(half_rot, dtype=jnp.float32) / rotary)
    phase_angle = jnp.arange(length, dtype=jnp.float32)[:, None] * inv_freq[None, :]
    return (jnp.cos(phase_angle), jnp.sin(phase_angle))

def rotate(values, cos_table, sin_table, rotary):
    half_rot = rotary // 2
    lead_part = values[..., :half_rot]
    tail_part = values[..., half_rot:rotary]
    cos_part = cos_table[:, None, :]
    sin_part = sin_table[:, None, :]
    return jnp.concatenate([lead_part * cos_part - tail_part * sin_part, tail_part * cos_part + lead_part * sin_part, values[..., rotary:]], axis=-1)

def layer_seq(seq_rows, seq_valid, params):
    norm1_gain, norm1_shift, qkv_matrix, qkv_shift, out_matrix, out_shift, norm2_gain, norm2_shift, up_matrix, up_shift, down_matrix, down_shift = params
    seq_len = seq_rows.shape[0]
    normed1 = low(layer_norm(seq_rows, norm1_gain, norm1_shift))
    projected = low_back(jnp.dot(normed1, qkv_matrix, precision=highest) + qkv_shift)
    projected = projected.reshape(seq_len, HEADS, 3, HEAD_DIM)
    cos_table, sin_table = rope_tables(seq_len, ROT)
    query_rows = low(rotate(projected[:, :, 0], cos_table, sin_table, ROT))
    key_rows = low(rotate(projected[:, :, 1], cos_table, sin_table, ROT))
    value_rows = low(projected[:, :, 2])
    positions = jnp.arange(seq_len, dtype=jnp.int32)
    earlier = positions[None, :] <= positions[:, None]
    itself = positions[None, :] == positions[:, None]
    allowed = earlier & ((seq_valid[None, :] > 0.5) | itself)
    scores = jnp.einsum('qhd,khd->hqk', query_rows, key_rows, precision=highest) * HEAD_DIM ** (-0.5)
    scores = low_back(scores)
    scores = jnp.where(allowed[None], scores, masked_score)
    row_max = lax.optimization_barrier(jnp.max(scores, axis=-1, keepdims=True))
    exp_scores = jnp.exp(scores - row_max)
    attn_probs = exp_scores / lax.optimization_barrier(jnp.sum(exp_scores, axis=-1, keepdims=True))
    attended = jnp.einsum('hqk,khd->qhd', low(attn_probs), value_rows, precision=highest)
    attended = low(low_back(attended)).reshape(seq_len, HEADS * HEAD_DIM)
    attn_out = jnp.dot(attended, out_matrix, precision=highest)
    normed2 = low(layer_norm(seq_rows, norm2_gain, norm2_shift))
    hidden = low_back(jnp.dot(normed2, up_matrix, precision=highest) + up_shift)
    activated = low(jax.nn.gelu(hidden, approximate=False))
    mlp_out = jnp.dot(activated, down_matrix, precision=highest)
    return seq_rows + seq_valid[:, None] * (attn_out + out_shift + mlp_out + down_shift)

def reference(tokens, lengths, valid_mask, ln1_gain, ln1_bias, qkv_weight, qkv_bias, out_weight, out_bias, ln2_gain, ln2_bias, up_weight, up_bias, down_weight, down_bias, out_grad):
    params = tuple((weight_arg.astype(jnp.float32) for weight_arg in (ln1_gain, ln1_bias, qkv_weight, qkv_bias, out_weight, out_bias, ln2_gain, ln2_bias, up_weight, up_bias, down_weight, down_bias)))
    positions = jnp.arange(SEQ_LEN, dtype=jnp.int32)
    validity = ((valid_mask.reshape(NSEQ, SEQ_LEN) == 1) & (positions[None, :] < lengths[:, None])).astype(jnp.float32)
    rows_all = tokens.astype(jnp.float32).reshape(NSEQ, SEQ_LEN, D)

    def forward(rows_in, weights_in):

        def per_sequence(carry, seq_item):
            return (carry, layer_seq(seq_item[0], seq_item[1], weights_in))
        _, outputs = lax.scan(jax.checkpoint(per_sequence), jnp.zeros((), jnp.float32), (rows_in, validity))
        return outputs
    outputs, pullback = jax.vjp(forward, rows_all, params)
    input_grad, param_grads = pullback(out_grad.astype(jnp.float32).reshape(NSEQ, SEQ_LEN, D))
    g_ln1, b_ln1, g_qkv, b_qkv, g_out, b_out, g_ln2, b_ln2, g_up, b_up, g_down, b_down = param_grads
    return (outputs.reshape(TOKENS, D).astype(jnp.bfloat16), input_grad.reshape(TOKENS, D).astype(jnp.bfloat16), g_ln1, b_ln1, g_qkv, b_qkv, g_out, b_out, g_ln2, b_ln2, g_up, b_up, g_down, b_down)
```

```python
from functools import partial

import jax
import jax.numpy as jnp
from jax import lax
from jax.sharding import PartitionSpec as P

HEAD_DIM = 256
SEQ_LEN = 2048
QBLOCK = 512
ROT = 64
BF16 = jnp.bfloat16
F32 = jnp.float32

norm_eps = 1e-05
rope_base = 10000.0
masked_score = -1e30


def layer_norm(rows):
    row_mean = jnp.mean(rows, axis=-1, keepdims=True)
    centred = rows - row_mean
    inv_std = lax.rsqrt(jnp.mean(centred * centred, axis=-1, keepdims=True) + norm_eps)
    return centred * inv_std, inv_std


def rope_tables(length, rotary):
    half_rot = rotary // 2
    inv_freq = rope_base ** (-2.0 * jnp.arange(half_rot, dtype=F32) / rotary)
    phase_angle = jnp.arange(length, dtype=F32)[:, None] * inv_freq[None, :]
    return (jnp.cos(phase_angle), jnp.sin(phase_angle))


def rotate(values, cos_table, sin_table, rotary):
    half_rot = rotary // 2
    lead_part = values[..., :half_rot]
    tail_part = values[..., half_rot:rotary]
    cos_part = cos_table[:, None, :]
    sin_part = sin_table[:, None, :]
    return jnp.concatenate(
        [
            lead_part * cos_part - tail_part * sin_part,
            tail_part * cos_part + lead_part * sin_part,
            values[..., rotary:],
        ],
        axis=-1,
    )


def allow_block(block_idx, key_end, seq_valid):
    query_pos = block_idx * QBLOCK + jnp.arange(QBLOCK)
    key_pos = jnp.arange(key_end)
    earlier = key_pos[None, :] <= query_pos[:, None]
    itself = key_pos[None, :] == query_pos[:, None]
    return earlier & (seq_valid[None, :key_end] | itself)


def block_scores(query_block, key_rows, allowed, score_scale):
    scores = (
        jnp.einsum("qhd,khd->hqk", query_block, key_rows, preferred_element_type=F32)
        * score_scale
    )
    return jnp.where(allowed[None], scores, masked_score)


def attend_forward(query_rows, key_rows, value_rows, seq_valid):
    seq_len = query_rows.shape[0]
    score_scale = query_rows.shape[-1] ** (-0.5)
    attended_list = []
    total_list = []
    for block_idx in range(seq_len // QBLOCK):
        key_end = (block_idx + 1) * QBLOCK
        allowed = allow_block(block_idx, key_end, seq_valid)
        scores = block_scores(
            query_rows[block_idx * QBLOCK : key_end], key_rows[:key_end], allowed, score_scale
        )
        row_max = jnp.max(scores, axis=-1, keepdims=True)
        exp_scores = jnp.exp(scores - row_max)
        row_total = jnp.sum(exp_scores, axis=-1, keepdims=True)
        attn_probs = (exp_scores / row_total).astype(BF16)
        attended = jnp.einsum(
            "hqk,khd->qhd", attn_probs, value_rows[:key_end], preferred_element_type=F32
        )
        attended_list.append(attended.astype(BF16))
        total_list.append(row_max[..., 0] + jnp.log(row_total[..., 0]))
    return (jnp.concatenate(attended_list, axis=0), jnp.concatenate(total_list, axis=1))


def attend_backward(query_rows, key_rows, value_rows, attended_grad, log_total, seq_valid):
    seq_len, head_count, head_dim = query_rows.shape
    score_scale = head_dim ** (-0.5)
    query_grad_list = []
    key_grad = jnp.zeros((seq_len, head_count, head_dim), F32)
    value_grad = jnp.zeros((seq_len, head_count, head_dim), F32)
    for block_idx in range(seq_len // QBLOCK):
        key_end = (block_idx + 1) * QBLOCK
        query_block = query_rows[block_idx * QBLOCK : key_end]
        grad_block = attended_grad[block_idx * QBLOCK : key_end]
        allowed = allow_block(block_idx, key_end, seq_valid)
        scores = block_scores(query_block, key_rows[:key_end], allowed, score_scale)
        attn_probs = jnp.exp(scores - log_total[:, block_idx * QBLOCK : key_end, None])
        probs_grad = jnp.einsum(
            "qhd,khd->hqk", grad_block, value_rows[:key_end], preferred_element_type=F32
        )
        row_dot = jnp.sum(attn_probs * probs_grad, axis=-1, keepdims=True)
        score_grad = (attn_probs * (probs_grad - row_dot)).astype(BF16)
        query_grad_list.append(
            jnp.einsum(
                "hqk,khd->qhd", score_grad, key_rows[:key_end], preferred_element_type=F32
            )
            * score_scale
        )
        pad_rows = ((0, seq_len - key_end), (0, 0), (0, 0))
        key_term = (
            jnp.einsum("hqk,qhd->khd", score_grad, query_block, preferred_element_type=F32)
            * score_scale
        )
        value_term = jnp.einsum(
            "hqk,qhd->khd",
            attn_probs.astype(BF16),
            grad_block,
            preferred_element_type=F32,
        )
        key_grad = key_grad + jnp.pad(key_term, pad_rows)
        value_grad = value_grad + jnp.pad(value_term, pad_rows)
    return (jnp.concatenate(query_grad_list, axis=0), key_grad, value_grad)


CORE = [(0, 1), (1, 0), (2, 3), (3, 2)]
YAX = [(0, 2), (2, 0), (1, 3), (3, 1)]
XAX = [(0, 1), (1, 0)]


def core_swap(block):
    return lax.ppermute(block, "tensor", CORE)


def y_swap(block):
    return lax.ppermute(block, "tensor", YAX)


def x_swap(block):
    return lax.ppermute(block, "branch", XAX)


def pick(array, index, size, axis=0):
    return lax.dynamic_slice_in_dim(array, index * size, size, axis)


def chain_gather(shard, place, count):
    buffer = jnp.zeros((3 * count - 2,) + shard.shape, shard.dtype)
    buffer = lax.dynamic_update_slice_in_dim(buffer, shard[None], place + count - 1, 0)
    right = left = shard
    for step in range(count - 1):
        right = lax.ppermute(right, "dp", [(k, k + 1) for k in range(step, count - 1)])
        left = lax.ppermute(left, "dp", [(k + 1, k) for k in range(count - 1 - step)])
        buffer = lax.dynamic_update_slice_in_dim(buffer, right[None], place - 1 - step + count - 1, 0)
        buffer = lax.dynamic_update_slice_in_dim(buffer, left[None], place + 1 + step + count - 1, 0)
    return buffer[count - 1 : 2 * count - 1]


def chain_reduce(piece, place, count):
    right = left = None
    for step in range(count - 1):
        right_send = piece(jnp.minimum(count - 1 - step + place, count - 1))
        left_send = piece(jnp.maximum(place - (count - 1 - step), 0))
        if right is not None:
            right_send = right_send.astype(F32) + right.astype(F32)
            left_send = left_send.astype(F32) + left.astype(F32)
        right = lax.ppermute(right_send.astype(BF16), "dp", [(k, k + 1) for k in range(step + 1)])
        left = lax.ppermute(
            left_send.astype(BF16), "dp", [(count - 1 - k, count - 2 - k) for k in range(step + 1)]
        )
    return piece(place).astype(F32) + right.astype(F32) + left.astype(F32)


def add16(first, second):
    return (first.astype(F32) + second.astype(F32)).astype(BF16)


def plane_reduce(part, core, why, ex):
    rows = part.shape[0]
    half, quarter, eighth, sixteenth = rows // 2, rows // 4, rows // 8, rows // 16
    mine = pick(part, core, half)
    mine = add16(mine, core_swap(pick(part, 1 - core, half)))
    first, second = mine[:quarter], mine[quarter:]
    first_next = y_swap(pick(first, 1 - why, eighth))
    second_next = x_swap(pick(second, 1 - ex, eighth))
    first = add16(pick(first, why, eighth), first_next)
    second = add16(pick(second, ex, eighth), second_next)
    first_next = x_swap(pick(first, 1 - ex, sixteenth))
    second_next = y_swap(pick(second, 1 - why, sixteenth))
    first = pick(first, ex, sixteenth).astype(F32) + first_next.astype(F32)
    second = pick(second, why, sixteenth).astype(F32) + second_next.astype(F32)
    return first, second


def own_rows(array, core, why, ex):
    rows = array.shape[0]
    sixteenth = rows // 16
    first = core * 8 + why * 2 + ex
    second = core * 8 + 4 + ex * 2 + why
    return pick(array, first, sixteenth), pick(array, second, sixteenth)


def join(low_index, mine, other, axis=0):
    return jnp.where(
        low_index == 0,
        jnp.concatenate([mine, other], axis),
        jnp.concatenate([other, mine], axis),
    )


def plane_gather(first, second, core, why, ex):
    first_next, second_next = x_swap(first), y_swap(second)
    first, second = join(ex, first, first_next), join(why, second, second_next)
    first_next, second_next = y_swap(first), x_swap(second)
    first, second = join(why, first, first_next), join(ex, second, second_next)
    mine = jnp.concatenate([first, second], 0)
    return join(core, mine, core_swap(mine))


def local(
    tokens,
    lengths,
    valid_mask,
    ln1_gain,
    ln1_bias,
    qkv_weight,
    qkv_bias,
    out_weight,
    out_bias,
    ln2_gain,
    ln2_bias,
    up_weight,
    up_bias,
    down_weight,
    down_bias,
    out_grad,
    *,
    count,
):
    row_count, width = tokens.shape
    seq_count = row_count // SEQ_LEN
    ex = lax.axis_index("branch")
    tensor_at = lax.axis_index("tensor")
    why, core = tensor_at // 2, tensor_at % 2
    place = lax.axis_index("dp")
    qkv_cols = qkv_bias.shape[0] // 2
    head_rows = out_weight.shape[0] // 2
    units = up_bias.shape[0] // 2
    head_count = qkv_cols // (3 * HEAD_DIM)
    chunk = width // (2 * count)

    qkv_full = chain_gather(pick(qkv_weight, ex, qkv_cols, 1), place, count).reshape(width, qkv_cols)
    out_full = chain_gather(pick(out_weight, ex, head_rows, 0), place, count)
    out_full = out_full.transpose(1, 0, 2).reshape(head_rows, width)
    up_full = chain_gather(pick(up_weight, ex, units, 1), place, count).reshape(width, units)
    down_full = chain_gather(pick(down_weight, ex, units, 0), place, count)
    down_full = down_full.transpose(1, 0, 2).reshape(units, width)

    positions = jnp.arange(SEQ_LEN, dtype=jnp.int32)
    seq_valid = (valid_mask.reshape(seq_count, SEQ_LEN) == 1) & (
        positions[None, :] < lengths[:, None]
    )
    validity = seq_valid.reshape(row_count).astype(F32)
    unit_rows, inv_std = layer_norm(tokens.astype(F32))
    grad_rows = out_grad * validity.astype(BF16)[:, None]
    normed1 = (unit_rows * ln1_gain + ln1_bias).astype(BF16)
    normed2 = (unit_rows * ln2_gain + ln2_bias).astype(BF16)
    cos_table, sin_table = rope_tables(SEQ_LEN, ROT)

    projected = jnp.dot(normed1, qkv_full, preferred_element_type=F32) + pick(qkv_bias, ex, qkv_cols)
    projected = projected.reshape(row_count, head_count, 3, HEAD_DIM)
    query_rows = rotate(projected[:, :, 0], cos_table, sin_table, ROT).astype(BF16)
    key_rows = rotate(projected[:, :, 1], cos_table, sin_table, ROT).astype(BF16)
    value_rows = projected[:, :, 2].astype(BF16)
    attended, log_total = attend_forward(query_rows, key_rows, value_rows, seq_valid[0])
    attended = attended.reshape(row_count, head_rows)
    out_partial = jnp.einsum("rc,rd->cd", attended, grad_rows, preferred_element_type=F32).astype(BF16)
    out_reduced = chain_reduce(
        lambda j: pick(out_partial.reshape(head_rows, 2, count, chunk), j, 1, 2), place, count
    )[:, :, 0]
    attended_grad = jnp.einsum("rd,cd->rc", grad_rows, out_full, preferred_element_type=F32).astype(BF16)
    query_grad, key_grad, value_grad = attend_backward(
        query_rows,
        key_rows,
        value_rows,
        attended_grad.reshape(row_count, head_count, HEAD_DIM),
        log_total,
        seq_valid[0],
    )
    query_grad = rotate(query_grad, cos_table, -sin_table, ROT)
    key_grad = rotate(key_grad, cos_table, -sin_table, ROT)
    qkv_grad = (
        jnp.stack([query_grad, key_grad, value_grad], axis=2).reshape(row_count, qkv_cols).astype(BF16)
    )
    qkv_partial = jnp.einsum("rd,rc->dc", normed1, qkv_grad, preferred_element_type=F32).astype(BF16)
    qkv_reduced = chain_reduce(
        lambda j: pick(qkv_partial.reshape(2, count, chunk, qkv_cols), j, 1, 1), place, count
    )[:, 0]
    qkv_bias_part = jnp.sum(qkv_grad, axis=0, dtype=F32)
    normed1_grad = jnp.einsum("rc,dc->rd", qkv_grad, qkv_full, preferred_element_type=F32)

    hidden = jnp.dot(normed2, up_full, preferred_element_type=F32) + pick(up_bias, ex, units)
    activated, gelu_back = jax.vjp(partial(jax.nn.gelu, approximate=False), hidden)
    activated = activated.astype(BF16)
    down_partial = jnp.einsum("rf,rd->fd", activated, grad_rows, preferred_element_type=F32).astype(BF16)
    down_reduced = chain_reduce(
        lambda j: pick(down_partial.reshape(units, 2, count, chunk), j, 1, 2), place, count
    )[:, :, 0]
    branch_part = jnp.dot(attended, out_full, preferred_element_type=F32)
    branch_part = branch_part + jnp.dot(activated, down_full, preferred_element_type=F32)
    branch_part = branch_part.astype(BF16)
    branch_first, branch_second = plane_reduce(branch_part, core, why, ex)

    activated_grad = jnp.einsum("rd,fd->rf", grad_rows, down_full, preferred_element_type=F32)
    hidden_grad = gelu_back(activated_grad)[0].astype(BF16)
    up_partial = jnp.einsum("rd,rf->df", normed2, hidden_grad, preferred_element_type=F32).astype(BF16)
    up_reduced = chain_reduce(
        lambda j: pick(up_partial.reshape(2, count, chunk, units), j, 1, 1), place, count
    )[:, 0]
    up_bias_part = jnp.sum(hidden_grad, axis=0, dtype=F32)
    normed2_grad = jnp.einsum("rf,df->rd", hidden_grad, up_full, preferred_element_type=F32)
    input_part = (normed1_grad * ln1_gain + normed2_grad * ln2_gain).astype(BF16)
    input_first, input_second = plane_reduce(input_part, core, why, ex)

    shift_sum = out_bias + down_bias
    tokens_own = own_rows(tokens, core, why, ex)
    validity_own = own_rows(validity, core, why, ex)
    out_grad_own = own_rows(out_grad, core, why, ex)

    def output_of(token_rows, valid_rows, total):
        return (token_rows.astype(F32) + valid_rows[:, None] * (total + shift_sum)).astype(BF16)

    output_rows = plane_gather(
        output_of(tokens_own[0], validity_own[0], branch_first),
        output_of(tokens_own[1], validity_own[1], branch_second),
        core,
        why,
        ex,
    )

    def input_of(token_rows, grad_own, total):
        unit_own, inv_own = layer_norm(token_rows.astype(F32))
        back = inv_own * (
            total
            - jnp.mean(total, axis=-1, keepdims=True)
            - unit_own * jnp.mean(total * unit_own, axis=-1, keepdims=True)
        )
        return (grad_own.astype(F32) + back).astype(BF16)

    grad_input = plane_gather(
        input_of(tokens_own[0], out_grad_own[0], input_first),
        input_of(tokens_own[1], out_grad_own[1], input_second),
        core,
        why,
        ex,
    )

    vectors = jnp.concatenate(
        [
            jnp.sum(normed1_grad * unit_rows, axis=0),
            jnp.sum(normed1_grad, axis=0),
            jnp.sum(normed2_grad * unit_rows, axis=0),
            jnp.sum(normed2_grad, axis=0),
            jnp.sum(grad_rows, axis=0, dtype=F32),
            qkv_bias_part,
            up_bias_part,
        ]
    ).reshape(-1, 128)
    hops = [
        lax.ppermute(vectors, "dp", [(k, (k + hop) % count) for k in range(count)])
        for hop in range(1, count)
    ]
    vectors = sum(hops, vectors)
    norm_rows, bias_rows = 4 * width // 128, width // 128
    norms, bias_grad, biases = (
        vectors[:norm_rows],
        vectors[norm_rows : norm_rows + bias_rows].reshape(width),
        vectors[norm_rows + bias_rows :],
    )
    for swap in (core_swap, y_swap, x_swap):
        norms = norms + swap(norms)
    norms = norms.reshape(4, width)
    other = x_swap(biases).reshape(-1)
    biases = biases.reshape(-1)
    qkv_bias_grad = join(ex, biases[:qkv_cols], other[:qkv_cols])
    up_bias_grad = join(ex, biases[qkv_cols:], other[qkv_cols:])

    def share(reduced, axis_of_pair, axis):
        mine = lax.dynamic_index_in_dim(reduced, ex, axis_of_pair, keepdims=False)
        given = lax.dynamic_index_in_dim(reduced, 1 - ex, axis_of_pair, keepdims=False)
        return join(ex, mine, x_swap(given.astype(BF16)).astype(F32), axis)

    return (
        output_rows,
        grad_input,
        norms[0],
        norms[1],
        share(qkv_reduced, 0, 1),
        qkv_bias_grad,
        share(out_reduced, 1, 0),
        bias_grad,
        norms[2],
        norms[3],
        share(up_reduced, 0, 1),
        up_bias_grad,
        share(down_reduced, 1, 0),
        bias_grad,
    )


def solution(mesh):
    return jax.shard_map(
        partial(local, count=mesh.shape["dp"]),
        mesh=mesh,
        in_specs=(
            P("dp", None),
            P("dp"),
            P("dp"),
            P(),
            P(),
            P("dp", "tensor"),
            P("tensor"),
            P("tensor", "dp"),
            P(),
            P(),
            P(),
            P("dp", "tensor"),
            P("tensor"),
            P("tensor", "dp"),
            P(),
            P("dp", None),
        ),
        out_specs=(
            P("dp", None),
            P("dp", None),
            P(),
            P(),
            P(("branch", "dp"), "tensor"),
            P("tensor"),
            P("tensor", ("branch", "dp")),
            P(),
            P(),
            P(),
            P(("branch", "dp"), "tensor"),
            P("tensor"),
            P("tensor", ("branch", "dp")),
            P(),
        ),
        check_vma=False,
    )
```

```python
from functools import partial

import jax
import jax.numpy as jnp
from jax import lax
from jax.experimental import pallas as pl
from jax.experimental.pallas import tpu as pltpu
from jax.sharding import PartitionSpec as P

HEAD_DIM = 256
SEQ_LEN = 2048
ROT = 64
LANES = 128
BF16 = jnp.bfloat16
F32 = jnp.float32

norm_eps = 1e-05
rope_base = 10000.0
masked_score = -1e30


def rope_tables(length, rotary):
    half_rot = rotary // 2
    inv_freq = rope_base ** (-2.0 * jnp.arange(half_rot, dtype=F32) / rotary)
    phase_angle = jnp.arange(length, dtype=F32)[:, None] * inv_freq[None, :]
    return (jnp.cos(phase_angle), jnp.sin(phase_angle))


def rope_back_cols(grad, cos_t, sin_t):
    half = ROT // 2
    lead, tail = grad[:half], grad[half:ROT]
    return jnp.concatenate(
        [lead * cos_t + tail * sin_t, tail * cos_t - lead * sin_t, grad[ROT:]], axis=0
    )


def nn(first, second):
    return lax.dot_general(first, second, (((1,), (0,)), ((), ())), preferred_element_type=F32)


def nt(first, second):
    return lax.dot_general(first, second, (((1,), (1,)), ((), ())), preferred_element_type=F32)


def project_kernel(rows_ref, weight_ref, bias_ref, cos_ref, ahead_ref, behind_ref, out_ref):
    out = nn(rows_ref[...], weight_ref[...]) + bias_ref[...]
    half = ROT // 2
    for part in range(2):
        base = part * HEAD_DIM
        lead = out[:, base : base + LANES]
        turned = (
            lead * cos_ref[...]
            + pltpu.roll(lead, LANES - half, 1) * ahead_ref[...]
            + pltpu.roll(lead, half, 1) * behind_ref[...]
        )
        scale = HEAD_DIM**-0.5 if part == 0 else 1.0
        out_ref[:, base : base + LANES] = (turned * scale).astype(BF16)
        rest = out[:, base + LANES : base + HEAD_DIM]
        out_ref[:, base + LANES : base + HEAD_DIM] = (rest * scale).astype(BF16)
    out_ref[:, 2 * HEAD_DIM :] = out[:, 2 * HEAD_DIM :].astype(BF16)


def params(limit=None):
    return pltpu.CompilerParams(dimension_semantics=("arbitrary",), vmem_limit_bytes=limit)


def cost(flops, bytes_accessed, transcendentals=0):
    return pl.CostEstimate(
        flops=flops // 1000, transcendentals=0, bytes_accessed=bytes_accessed // 1000
    )


def project(rows, weight, bias, tables, block=512):
    count, width = rows.shape
    cols = bias.shape[1]
    table_spec = pl.BlockSpec((block, LANES), lambda i: (i, 0))
    return pl.pallas_call(
        project_kernel,
        grid=(count // block,),
        in_specs=[
            pl.BlockSpec((block, width), lambda i: (i, 0)),
            pl.BlockSpec((width, cols), lambda i: (0, 0)),
            pl.BlockSpec((1, cols), lambda i: (0, 0)),
            table_spec,
            table_spec,
            table_spec,
        ],
        out_specs=pl.BlockSpec((block, cols), lambda i: (i, 0)),
        out_shape=jax.ShapeDtypeStruct((count, cols), BF16),
        compiler_params=params(),
        cost_estimate=cost(2 * count * width * cols, 2 * (count * width + width * cols + count * cols)),
        name="project",
    )(rows, weight, bias, *tables)


def spread(column, width):
    return jnp.concatenate([column] * (width // LANES), axis=1)


def masked(scores, bias, block_idx, block):
    start = block_idx * block
    own = scores[start:]
    key_at = lax.broadcasted_iota(jnp.int32, own.shape, 0)
    query_at = lax.broadcasted_iota(jnp.int32, own.shape, 1)
    shift = spread(bias, block)
    own = jnp.where(
        key_at < query_at, own + shift[start:], jnp.where(key_at == query_at, own, masked_score)
    )
    if block_idx == 0:
        return own
    return jnp.concatenate([scores[:start] + shift[:start], own], axis=0)


def attend_kernel(query_ref, key_ref, value_ref, bias_ref, out_ref, total_ref, value_t, *, block):
    at = pl.program_id(0)

    @pl.when(at == 0)
    def _():
        value_t[...] = value_ref[...].T

    for block_idx in range(key_ref.shape[0] // block):

        @pl.when(at == block_idx)
        def _(block_idx=block_idx):
            end = (block_idx + 1) * block
            scores = masked(
                nt(key_ref[:end], query_ref[...]), bias_ref[:end], block_idx, block
            )
            top = jnp.max(scores, axis=0, keepdims=True)
            weights = jnp.exp(scores - top)
            total = jnp.sum(weights, axis=0, keepdims=True)
            out = nn(value_t[:, :end], weights.astype(BF16)) / total
            out_ref[...] = out.T.astype(BF16)
            total_ref[...] = jnp.broadcast_to(top + jnp.log(total), total_ref.shape)


def attend(qkv, bias, block=512):
    count = qkv.shape[0]
    pairs = count * (count + block) // 2
    return pl.pallas_call(
        partial(attend_kernel, block=block),
        grid=(count // block,),
        in_specs=[
            pl.BlockSpec((block, HEAD_DIM), lambda i: (i, 0)),
            pl.BlockSpec((count, HEAD_DIM), lambda i: (0, 1)),
            pl.BlockSpec((count, HEAD_DIM), lambda i: (0, 2)),
            pl.BlockSpec((count, LANES), lambda i: (0, 0)),
        ],
        out_specs=[
            pl.BlockSpec((block, HEAD_DIM), lambda i: (i, 0)),
            pl.BlockSpec((8, block), lambda i: (0, i)),
        ],
        out_shape=[
            jax.ShapeDtypeStruct((count, HEAD_DIM), BF16),
            jax.ShapeDtypeStruct((8, count), F32),
        ],
        scratch_shapes=[pltpu.VMEM((HEAD_DIM, count), BF16)],
        compiler_params=params(),
        cost_estimate=cost(4 * pairs * HEAD_DIM, 8 * count * HEAD_DIM, pairs),
        name="attend",
    )(qkv, qkv, qkv, bias)


def attend_back_kernel(
    query_ref, key_ref, value_ref, grad_ref, total_ref, bias_ref, cos_ref, sin_ref,
    out_ref, sums_ref, key_t, key_grad, value_grad, *, block
):
    at = pl.program_id(0)
    count = key_ref.shape[0]
    blocks = count // block

    @pl.when(at == 0)
    def _():
        key_t[...] = key_ref[...].T
        key_grad[...] = jnp.zeros_like(key_grad)
        value_grad[...] = jnp.zeros_like(value_grad)
        sums_ref[...] = jnp.zeros_like(sums_ref)

    for block_idx in range(blocks):

        @pl.when(at == block_idx)
        def _(block_idx=block_idx):
            start, end = block_idx * block, (block_idx + 1) * block
            query, grad = query_ref[...], grad_ref[...]
            scores = masked(nt(key_ref[:end], query), bias_ref[:end], block_idx, block)
            probs = jnp.exp(scores - total_ref[0:1])
            probs_grad = nt(value_ref[:end], grad)
            dots = jnp.sum(probs * probs_grad, axis=0, keepdims=True)
            score_grad = (probs * (probs_grad - dots)).astype(BF16)
            value_grad[:end] += nn(probs.astype(BF16), grad)
            key_grad[:end] += nn(score_grad, query)
            query_grad = nn(key_t[:, :end], score_grad) * (HEAD_DIM**-0.5)
            query_grad = rope_back_cols(
                query_grad, cos_ref[:, start:end], sin_ref[:, start:end]
            ).T.astype(BF16)
            out_ref[start:end, :HEAD_DIM] = query_grad
            sums_ref[:, :HEAD_DIM] += jnp.sum(query_grad.astype(F32), axis=0, keepdims=True)

    @pl.when(at == blocks - 1)
    def _():
        turned = rope_back_cols(key_grad[...].T, cos_ref[...], sin_ref[...]).T.astype(BF16)
        out_ref[:, HEAD_DIM : 2 * HEAD_DIM] = turned
        sums_ref[:, HEAD_DIM : 2 * HEAD_DIM] = jnp.sum(turned.astype(F32), axis=0, keepdims=True)
        low = value_grad[...].astype(BF16)
        out_ref[:, 2 * HEAD_DIM :] = low
        sums_ref[:, 2 * HEAD_DIM :] = jnp.sum(low.astype(F32), axis=0, keepdims=True)


def attend_back(qkv, grad, total, bias, cos_t, sin_t, block=512):
    count = qkv.shape[0]
    pairs = count * (count + block) // 2
    half = ROT // 2
    return pl.pallas_call(
        partial(attend_back_kernel, block=block),
        grid=(count // block,),
        in_specs=[
            pl.BlockSpec((block, HEAD_DIM), lambda i: (i, 0)),
            pl.BlockSpec((count, HEAD_DIM), lambda i: (0, 1)),
            pl.BlockSpec((count, HEAD_DIM), lambda i: (0, 2)),
            pl.BlockSpec((block, HEAD_DIM), lambda i: (i, 0)),
            pl.BlockSpec((8, block), lambda i: (0, i)),
            pl.BlockSpec((count, LANES), lambda i: (0, 0)),
            pl.BlockSpec((half, count), lambda i: (0, 0)),
            pl.BlockSpec((half, count), lambda i: (0, 0)),
        ],
        out_specs=[
            pl.BlockSpec((count, 3 * HEAD_DIM), lambda i: (0, 0)),
            pl.BlockSpec((1, 3 * HEAD_DIM), lambda i: (0, 0)),
        ],
        out_shape=[
            jax.ShapeDtypeStruct((count, 3 * HEAD_DIM), BF16),
            jax.ShapeDtypeStruct((1, 3 * HEAD_DIM), F32),
        ],
        scratch_shapes=[
            pltpu.VMEM((HEAD_DIM, count), BF16),
            pltpu.VMEM((count, HEAD_DIM), F32),
            pltpu.VMEM((count, HEAD_DIM), F32),
        ],
        compiler_params=params(),
        cost_estimate=cost(10 * pairs * HEAD_DIM, 16 * count * HEAD_DIM, pairs),
        name="attend_back",
    )(qkv, qkv, qkv, grad, total, bias, cos_t, sin_t)


def up_kernel(rows_ref, weight_ref, bias_ref, act_ref, slope_ref, *, chunk):
    rows = rows_ref[...]
    for at in range(0, weight_ref.shape[1], chunk):
        span = slice(at, at + chunk)
        hidden = nn(rows, weight_ref[:, span]) + bias_ref[:, span]
        share = 0.5 + 0.5 * lax.erf(hidden * 0.7071067811865476)
        density = jnp.exp(hidden * hidden * -0.5) * 0.3989422804014327
        act_ref[:, span] = (hidden * share).astype(BF16)
        slope_ref[:, span] = (share + hidden * density).astype(slope_ref.dtype)


def up_gelu(rows, weight, bias, block=256, chunk=256):
    count, width = rows.shape
    units = weight.shape[1]
    out_spec = pl.BlockSpec((block, units), lambda i: (i, 0))
    return pl.pallas_call(
        partial(up_kernel, chunk=chunk),
        grid=(count // block,),
        in_specs=[
            pl.BlockSpec((block, width), lambda i: (i, 0)),
            pl.BlockSpec((width, units), lambda i: (0, 0)),
            pl.BlockSpec((1, units), lambda i: (0, 0)),
        ],
        out_specs=[out_spec, out_spec],
        out_shape=[
            jax.ShapeDtypeStruct((count, units), BF16),
            jax.ShapeDtypeStruct((count, units), F32),
        ],
        compiler_params=params(),
        cost_estimate=cost(
            2 * count * width * units, 2 * (count * width + width * units + 3 * count * units), count * units
        ),
        name="up_gelu",
    )(rows, weight, bias)


def slope_kernel(grad_ref, weight_ref, slope_ref, out_ref, sums_ref, *, chunk):
    @pl.when(pl.program_id(0) == 0)
    def _():
        sums_ref[...] = jnp.zeros_like(sums_ref)

    grad = grad_ref[...]
    for at in range(0, weight_ref.shape[1], chunk):
        span = slice(at, at + chunk)
        low = (nn(grad, weight_ref[:, span]) * slope_ref[:, span]).astype(BF16)
        out_ref[:, span] = low
        sums_ref[:, span] += jnp.sum(low.astype(F32), axis=0, keepdims=True)


def hidden_back(grad, weight, slope, block=256, chunk=256):
    count, width = grad.shape
    units = weight.shape[1]
    return pl.pallas_call(
        partial(slope_kernel, chunk=chunk),
        grid=(count // block,),
        in_specs=[
            pl.BlockSpec((block, width), lambda i: (i, 0)),
            pl.BlockSpec((width, units), lambda i: (0, 0)),
            pl.BlockSpec((block, units), lambda i: (i, 0)),
        ],
        out_specs=[
            pl.BlockSpec((block, units), lambda i: (i, 0)),
            pl.BlockSpec((1, units), lambda i: (0, 0)),
        ],
        out_shape=[
            jax.ShapeDtypeStruct((count, units), BF16),
            jax.ShapeDtypeStruct((1, units), F32),
        ],
        compiler_params=params(),
        cost_estimate=cost(2 * count * width * units, 2 * (count * width + width * units + 3 * count * units)),
        name="hidden_back",
    )(grad, weight, slope)


def dgrad_sums(grad_ref, weight_ref, rows_ref, mean, inv, dot_ref, sum_ref, span):
    normed = nt(grad_ref[...], weight_ref[span])
    unit = (rows_ref[:, span].astype(F32) - mean) * inv
    dot_ref[:, span] += jnp.sum(normed * unit, axis=0, keepdims=True)
    sum_ref[:, span] += jnp.sum(normed, axis=0, keepdims=True)
    return normed


def dgrad_first_kernel(
    grad_ref, weight_ref, rows_ref, mean_ref, inv_ref, gain_ref, out_ref, dot_ref, sum_ref, *, chunk
):
    @pl.when(pl.program_id(0) == 0)
    def _():
        dot_ref[...] = jnp.zeros_like(dot_ref)
        sum_ref[...] = jnp.zeros_like(sum_ref)

    mean, inv = mean_ref[...], inv_ref[...]
    for at in range(0, weight_ref.shape[0], chunk):
        span = slice(at, at + chunk)
        normed = dgrad_sums(grad_ref, weight_ref, rows_ref, mean, inv, dot_ref, sum_ref, span)
        out_ref[:, span] = normed * gain_ref[:, span]


def dgrad_half_kernel(
    half_ref, grad_ref, weight_ref, rows_ref, mean_ref, inv_ref, gain_ref, before_ref,
    out_ref, dot_ref, sum_ref, *, chunk
):
    @pl.when(pl.program_id(0) == 0)
    def _():
        dot_ref[...] = jnp.zeros_like(dot_ref)
        sum_ref[...] = jnp.zeros_like(sum_ref)

    mean, inv = mean_ref[...], inv_ref[...]
    for at in range(0, weight_ref.shape[0], chunk):
        span = slice(at, at + chunk)
        normed = dgrad_sums(grad_ref, weight_ref, rows_ref, mean, inv, dot_ref, sum_ref, span)
        out_ref[:, span] = (normed * gain_ref[:, span] + before_ref[:, span]).astype(BF16)


def dgrad_first(grad, weight, rows, mean, inv, gain, block=256, chunk=256):
    count, width = rows.shape
    cols = grad.shape[1]
    wide = pl.BlockSpec((block, width), lambda i: (i, 0))
    thin = pl.BlockSpec((block, 1), lambda i: (i, 0))
    vector = pl.BlockSpec((1, width), lambda i: (0, 0))
    return pl.pallas_call(
        partial(dgrad_first_kernel, chunk=chunk),
        grid=(count // block,),
        in_specs=[
            pl.BlockSpec((block, cols), lambda i: (i, 0)),
            pl.BlockSpec((width, cols), lambda i: (0, 0)),
            wide,
            thin,
            thin,
            vector,
        ],
        out_specs=[wide, vector, vector],
        out_shape=[
            jax.ShapeDtypeStruct((count, width), F32),
            jax.ShapeDtypeStruct((1, width), F32),
            jax.ShapeDtypeStruct((1, width), F32),
        ],
        compiler_params=params(),
        cost_estimate=cost(2 * count * width * cols, 6 * count * width + 2 * width * cols),
        name="dgrad_first",
    )(grad, weight, rows, mean, inv, gain)


def dgrad_half(half, grad, weight, rows, mean, inv, gain, before, block=256, chunk=256):
    count, width = rows.shape
    cols = grad.shape[1]
    steps = count // block // 2
    wide = pl.BlockSpec((block, width), lambda i, h: (h[0] * steps + i, 0))
    thin = pl.BlockSpec((block, 1), lambda i, h: (h[0] * steps + i, 0))
    vector = pl.BlockSpec((1, width), lambda i, h: (0, 0))
    return pl.pallas_call(
        partial(dgrad_half_kernel, chunk=chunk),
        grid_spec=pltpu.PrefetchScalarGridSpec(
            num_scalar_prefetch=1,
            grid=(steps,),
            in_specs=[
                pl.BlockSpec((block, cols), lambda i, h: (h[0] * steps + i, 0)),
                pl.BlockSpec((width, cols), lambda i, h: (0, 0)),
                wide,
                thin,
                thin,
                vector,
                wide,
            ],
            out_specs=[pl.BlockSpec((block, width), lambda i, h: (i, 0)), vector, vector],
        ),
        out_shape=[
            jax.ShapeDtypeStruct((count // 2, width), BF16),
            jax.ShapeDtypeStruct((1, width), F32),
            jax.ShapeDtypeStruct((1, width), F32),
        ],
        compiler_params=params(),
        cost_estimate=cost(count * width * cols, 3 * count * width + 2 * width * cols),
        name="dgrad_half",
    )(half.reshape(1), grad, weight, rows, mean, inv, gain, before)


def branch_kernel(half_ref, heads_ref, out_ref_w, act_ref, down_ref, out_ref, *, chunk):
    heads, act = heads_ref[...], act_ref[...]
    for at in range(0, down_ref.shape[0], chunk):
        span = slice(at, at + chunk)
        out_ref[:, span] = (nt(heads, out_ref_w[span]) + nt(act, down_ref[span])).astype(BF16)


def branch_half(half, heads, pack, act, down, block=256, chunk=256):
    count = heads.shape[0]
    width, units = down.shape
    head_rows = heads.shape[1]
    last = pack.shape[1] // head_rows - 1
    steps = count // block // 2
    return pl.pallas_call(
        partial(branch_kernel, chunk=chunk),
        grid_spec=pltpu.PrefetchScalarGridSpec(
            num_scalar_prefetch=1,
            grid=(steps,),
            in_specs=[
                pl.BlockSpec((block, head_rows), lambda i, h: (h[0] * steps + i, 0)),
                pl.BlockSpec((width, head_rows), lambda i, h: (0, last)),
                pl.BlockSpec((block, units), lambda i, h: (h[0] * steps + i, 0)),
                pl.BlockSpec((width, units), lambda i, h: (0, 0)),
            ],
            out_specs=pl.BlockSpec((block, width), lambda i, h: (i, 0)),
        ),
        out_shape=jax.ShapeDtypeStruct((count // 2, width), BF16),
        compiler_params=params(),
        cost_estimate=cost(count * width * (units + head_rows), count * width + 2 * width * units + count * units),
        name="branch_half",
    )(half.reshape(1), heads, pack, act, down)


CORE = [(0, 1), (1, 0), (2, 3), (3, 2)]
YAX = [(0, 2), (2, 0), (1, 3), (3, 1)]
XAX = [(0, 1), (1, 0)]


def core_swap(block):
    return lax.ppermute(block, "tensor", CORE)


def y_swap(block):
    return lax.ppermute(block, "tensor", YAX)


def x_swap(block):
    return lax.ppermute(block, "branch", XAX)


def pick(array, index, size, axis=0):
    return lax.dynamic_slice_in_dim(array, index * size, size, axis)


def add16(first, second):
    return (first.astype(F32) + second.astype(F32)).astype(BF16)


def own_rows(array, core, why, ex):
    rows = array.shape[0]
    sixteenth = rows // 16
    first = core * 8 + why * 2 + ex
    second = core * 8 + 4 + ex * 2 + why
    return pick(array, first, sixteenth), pick(array, second, sixteenth)


def join(low_index, mine, other, axis=0):
    return jnp.where(
        low_index == 0,
        jnp.concatenate([mine, other], axis),
        jnp.concatenate([other, mine], axis),
    )


def plane_gather(first, second, core, why, ex):
    first_next, second_next = x_swap(first), y_swap(second)
    first, second = join(ex, first, first_next), join(why, second, second_next)
    first_next, second_next = y_swap(first), x_swap(second)
    first, second = join(why, first, first_next), join(ex, second, second_next)
    mine = jnp.concatenate([first, second], 0)
    return join(core, mine, core_swap(mine))


def after(value, *first):
    return lax.optimization_barrier((value,) + first)[0]


def reduce_sends(piece, place, count, step, got):
    right = piece(jnp.minimum(count - 1 - step + place, count - 1))
    left = piece(jnp.maximum(place - (count - 1 - step), 0))
    if got is None:
        return right, left
    return add16(right, got[0]), add16(left, got[1])


def reduce_hop(sends, count, step):
    return (
        lax.ppermute(sends[0], "dp", [(k, k + 1) for k in range(step + 1)]),
        lax.ppermute(sends[1], "dp", [(count - 1 - k, count - 2 - k) for k in range(step + 1)]),
    )


def reduced(piece, place, got):
    right, left = got
    return piece(place).astype(F32) + right.astype(F32) + left.astype(F32)


def halving_send(keep, got, why, ex):
    quarter = keep.shape[0] // 2
    eighth = quarter // 2
    first = add16(
        pick(keep[:quarter], 1 - why, eighth), pick(got[:quarter], 1 - why, eighth)
    )
    second = add16(pick(keep[quarter:], 1 - ex, eighth), pick(got[quarter:], 1 - ex, eighth))
    return first, second


def halving_rest(keep, got, two, why, ex):
    quarter = keep.shape[0] // 2
    eighth, sixteenth = quarter // 2, quarter // 4

    def mine(start, index, received):
        rows = slice(start, start + quarter)
        return (
            pick(keep[rows], index, eighth).astype(F32)
            + pick(got[rows], index, eighth).astype(F32)
            + received.astype(F32)
        )

    first, second = mine(0, why, two[0]), mine(quarter, ex, two[1])
    first_got = x_swap(pick(first, 1 - ex, sixteenth).astype(BF16))
    second_got = y_swap(pick(second, 1 - why, sixteenth).astype(BF16))
    return (
        pick(first, ex, sixteenth) + first_got.astype(F32),
        pick(second, why, sixteenth) + second_got.astype(F32),
    )


def weight_grad(rows, cols):
    return jnp.einsum("rd,rc->dc", rows, cols, preferred_element_type=F32).astype(BF16)


def local(
    tokens,
    lengths,
    valid_mask,
    ln1_gain,
    ln1_bias,
    qkv_weight,
    qkv_bias,
    out_weight,
    out_bias,
    ln2_gain,
    ln2_bias,
    up_weight,
    up_bias,
    down_weight,
    down_bias,
    out_grad,
    *,
    count,
):
    row_count, width = tokens.shape
    ex = lax.axis_index("branch")
    tensor_at = lax.axis_index("tensor")
    why, core = tensor_at // 2, tensor_at % 2
    place = lax.axis_index("dp")
    qkv_cols = qkv_bias.shape[0] // 2
    head_rows = out_weight.shape[0] // 2
    units = up_bias.shape[0] // 2
    chunk = width // (2 * count)

    heads_shard = jnp.concatenate(
        [pick(qkv_weight, ex, qkv_cols, 1), pick(out_weight, ex, head_rows, 0).T], axis=1
    )
    up_shard = pick(up_weight, ex, units, 1)
    down_shard = pick(down_weight, ex, units, 0).T
    heads_full = lax.all_gather(heads_shard, "dp", axis=0, tiled=True)
    up_full = lax.all_gather(up_shard, "dp", axis=0, tiled=True)
    down_full = lax.all_gather(down_shard, "dp", axis=0, tiled=True)

    positions = jnp.arange(row_count, dtype=jnp.int32)
    seq_valid = (valid_mask == 1) & (positions < lengths[0])
    validity = seq_valid.astype(F32)
    key_bias = jnp.broadcast_to(
        jnp.where(seq_valid, 0.0, masked_score)[:, None], (row_count, LANES)
    )
    rows_f32 = tokens.astype(F32)
    mean = jnp.mean(rows_f32, axis=-1, keepdims=True)
    centred = rows_f32 - mean
    inv_std = lax.rsqrt(jnp.mean(centred * centred, axis=-1, keepdims=True) + norm_eps)
    unit_rows = centred * inv_std
    grad_rows = out_grad * validity.astype(BF16)[:, None]
    normed1 = (unit_rows * ln1_gain + ln1_bias).astype(BF16)
    normed2 = (unit_rows * ln2_gain + ln2_bias).astype(BF16)
    cos_table, sin_table = rope_tables(row_count, ROT)
    gap = jnp.zeros((row_count, ROT // 2), F32)
    rest = jnp.zeros((row_count, LANES - ROT), F32)
    tables = (
        jnp.concatenate([cos_table, cos_table, rest + 1.0], axis=1),
        jnp.concatenate([-sin_table, gap, rest], axis=1),
        jnp.concatenate([gap, sin_table, rest], axis=1),
    )

    qkv = project(normed1, heads_full, pick(qkv_bias, ex, qkv_cols)[None], tables)
    attended, log_total = attend(qkv, key_bias)
    attended_grad = jnp.dot(
        grad_rows, heads_full[:, qkv_cols:], preferred_element_type=F32
    ).astype(BF16)
    out_partial = weight_grad(grad_rows, attended)
    attended_grad = after(attended_grad, out_partial)
    qkv_grad, qkv_bias_part = attend_back(
        qkv, attended_grad, log_total, key_bias, cos_table.T, sin_table.T
    )
    qkv_partial = weight_grad(normed1, qkv_grad)

    def split(partial_sum, at):
        return pick(partial_sum.reshape(2, count, chunk, -1), at, 1, 1)[:, 0]

    def heads_piece(at):
        return jnp.concatenate([split(qkv_partial, at), split(out_partial, at)], axis=-1)

    def run_hops(piece, got, first, last):
        for step in range(first, last):
            got = reduce_hop(reduce_sends(piece, place, count, step, got), count, step)
        return got

    hops_a, hops_b = (count - 1) // 3, 2 * (count - 1) // 3
    got = run_hops(heads_piece, None, 0, hops_a - 1)
    sends = reduce_sends(heads_piece, place, count, hops_a - 1, got)
    got = reduce_hop(sends, count, hops_a - 1)
    input_part, dot1, sum1 = dgrad_first(
        after(qkv_grad, *sends), heads_full, tokens, mean, inv_std, ln1_gain[None]
    )
    got = after(got, input_part)
    got = run_hops(heads_piece, got, hops_a, hops_b - 1)
    sends = reduce_sends(heads_piece, place, count, hops_b - 1, got)
    got = reduce_hop(sends, count, hops_b - 1)
    activated, slope = up_gelu(
        after(normed2, input_part, *sends), up_full, pick(up_bias, ex, units)[None]
    )
    got = after(got, activated)
    got = run_hops(heads_piece, got, hops_b, count - 2)
    sends = reduce_sends(heads_piece, place, count, count - 2, got)
    got = reduce_hop(sends, count, count - 2)
    down_partial = weight_grad(after(grad_rows, activated, *sends), activated)

    def scatter(partial_sum):
        return lax.psum_scatter(
            partial_sum.reshape(2, width // 2, -1), "dp", scatter_dimension=1, tiled=True
        )

    down_total = scatter(down_partial)
    got = after(got, down_partial)
    heads_total = reduced(heads_piece, place, got)

    branch_send = branch_half(
        1 - core, attended, heads_full, after(activated, down_partial, heads_total), down_full
    )
    branch_core = core_swap(branch_send)
    branch_keep = branch_half(core, attended, heads_full, after(activated, branch_send), down_full)
    branch_core = after(branch_core, branch_keep)
    branch_two = halving_send(branch_keep, branch_core, why, ex)
    branch_two_got = y_swap(branch_two[0]), x_swap(branch_two[1])
    hidden_grad, up_bias_part = hidden_back(
        after(grad_rows, branch_keep, *branch_two), down_full, slope
    )
    norm_rows = tokens, mean, inv_std, ln2_gain[None], input_part
    input_send, dot2, sum2 = dgrad_half(1 - core, hidden_grad, up_full, *norm_rows)
    input_core = core_swap(input_send)
    input_keep, dot3, sum3 = dgrad_half(core, after(hidden_grad, input_send), up_full, *norm_rows)
    dot2, sum2 = dot2 + dot3, sum2 + sum3
    input_core = after(input_core, input_keep)
    input_two = halving_send(input_keep, input_core, why, ex)
    input_two_got = y_swap(input_two[0]), x_swap(input_two[1])
    branch_two_got = after(branch_two_got, input_keep)
    up_partial = weight_grad(after(normed2, input_keep, *input_two), hidden_grad)
    up_total = scatter(up_partial)
    branch_first, branch_second = halving_rest(branch_keep, branch_core, branch_two_got, why, ex)
    input_first, input_second = halving_rest(input_keep, input_core, input_two_got, why, ex)

    shift_sum = out_bias + down_bias
    tokens_own = own_rows(tokens, core, why, ex)
    validity_own = own_rows(validity, core, why, ex)
    out_grad_own = own_rows(out_grad, core, why, ex)
    mean_own = own_rows(mean, core, why, ex)
    inv_own = own_rows(inv_std, core, why, ex)

    def output_of(at, total):
        return (
            tokens_own[at].astype(F32) + validity_own[at][:, None] * (total + shift_sum)
        ).astype(BF16)

    output_rows = plane_gather(
        output_of(0, branch_first), output_of(1, branch_second), core, why, ex
    )

    def input_of(at, total):
        unit = (tokens_own[at].astype(F32) - mean_own[at]) * inv_own[at]
        back = inv_own[at] * (
            total
            - jnp.mean(total, axis=-1, keepdims=True)
            - unit * jnp.mean(total * unit, axis=-1, keepdims=True)
        )
        return (out_grad_own[at].astype(F32) + back).astype(BF16)

    grad_input = plane_gather(
        input_of(0, input_first), input_of(1, input_second), core, why, ex
    )

    vectors = jnp.concatenate(
        [
            dot1[0],
            sum1[0],
            dot2[0],
            sum2[0],
            jnp.sum(grad_rows, axis=0, dtype=F32),
            qkv_bias_part[0],
            up_bias_part[0],
        ]
    ).reshape(-1, LANES)
    hops = [
        lax.ppermute(vectors, "dp", [(k, (k + hop) % count) for k in range(count)])
        for hop in range(1, count)
    ]
    vectors = sum(hops, vectors)
    norm_rows, bias_rows = 4 * width // LANES, width // LANES
    norms, bias_grad, biases = (
        vectors[:norm_rows],
        vectors[norm_rows : norm_rows + bias_rows].reshape(width),
        vectors[norm_rows + bias_rows :],
    )
    for swap in (core_swap, y_swap, x_swap):
        norms = norms + swap(norms)
    norms = norms.reshape(4, width)
    other = x_swap(biases).reshape(-1)
    biases = biases.reshape(-1)
    qkv_bias_grad = join(ex, biases[:qkv_cols], other[:qkv_cols])
    up_bias_grad = join(ex, biases[qkv_cols:], other[qkv_cols:])

    def share(total):
        mine = lax.dynamic_index_in_dim(total, ex, 0, keepdims=False)
        given = lax.dynamic_index_in_dim(total, 1 - ex, 0, keepdims=False)
        return mine.astype(F32), x_swap(given.astype(BF16)).astype(F32)

    mine, other = share(heads_total)
    qkv_out = join(ex, mine[:, :qkv_cols], other[:, :qkv_cols], 1)
    out_out = join(ex, mine[:, qkv_cols:].T, other[:, qkv_cols:].T, 0)
    mine, other = share(down_total)
    down_out = join(ex, mine.T, other.T, 0)
    mine, other = share(up_total)
    up_out = join(ex, mine, other, 1)

    return (
        output_rows,
        grad_input,
        norms[0],
        norms[1],
        qkv_out,
        qkv_bias_grad,
        out_out,
        bias_grad,
        norms[2],
        norms[3],
        up_out,
        up_bias_grad,
        down_out,
        bias_grad,
    )


def solution(mesh):
    return jax.shard_map(
        partial(local, count=mesh.shape["dp"]),
        mesh=mesh,
        in_specs=(
            P("dp", None),
            P("dp"),
            P("dp"),
            P(),
            P(),
            P("dp", "tensor"),
            P("tensor"),
            P("tensor", "dp"),
            P(),
            P(),
            P(),
            P("dp", "tensor"),
            P("tensor"),
            P("tensor", "dp"),
            P(),
            P("dp", None),
        ),
        out_specs=(
            P("dp", None),
            P("dp", None),
            P(),
            P(),
            P(("branch", "dp"), "tensor"),
            P("tensor"),
            P("tensor", ("branch", "dp")),
            P(),
            P(),
            P(),
            P(("branch", "dp"), "tensor"),
            P("tensor"),
            P("tensor", ("branch", "dp")),
            P(),
        ),
        check_vma=False,
    )
```

```python
from functools import partial

import jax
import jax.numpy as jnp
from jax import lax
from jax.experimental import pallas as pl
from jax.experimental.pallas import tpu as pltpu
from jax.sharding import PartitionSpec as P

HEAD_DIM = 256
SEQ_LEN = 2048
ROT = 64
LANES = 128
BF16 = jnp.bfloat16
F32 = jnp.float32

norm_eps = 1e-05
rope_base = 10000.0
masked_score = -1e30


def rope_tables(length, rotary):
    half_rot = rotary // 2
    inv_freq = rope_base ** (-2.0 * jnp.arange(half_rot, dtype=F32) / rotary)
    phase_angle = jnp.arange(length, dtype=F32)[:, None] * inv_freq[None, :]
    return (jnp.cos(phase_angle), jnp.sin(phase_angle))


def rope_back_cols(grad, cos_t, sin_t):
    half = ROT // 2
    lead, tail = grad[:half], grad[half:ROT]
    return jnp.concatenate(
        [lead * cos_t + tail * sin_t, tail * cos_t - lead * sin_t, grad[ROT:]], axis=0
    )


def nn(first, second):
    return lax.dot_general(first, second, (((1,), (0,)), ((), ())), preferred_element_type=F32)


def nt(first, second):
    return lax.dot_general(first, second, (((1,), (1,)), ((), ())), preferred_element_type=F32)


def project_kernel(rows_ref, weight_ref, bias_ref, cos_ref, ahead_ref, behind_ref, out_ref):
    out = nn(rows_ref[...], weight_ref[...]) + bias_ref[...]
    half = ROT // 2
    for part in range(2):
        base = part * HEAD_DIM
        lead = out[:, base : base + LANES]
        turned = (
            lead * cos_ref[...]
            + pltpu.roll(lead, LANES - half, 1) * ahead_ref[...]
            + pltpu.roll(lead, half, 1) * behind_ref[...]
        )
        scale = HEAD_DIM**-0.5 if part == 0 else 1.0
        out_ref[:, base : base + LANES] = (turned * scale).astype(BF16)
        rest = out[:, base + LANES : base + HEAD_DIM]
        out_ref[:, base + LANES : base + HEAD_DIM] = (rest * scale).astype(BF16)
    out_ref[:, 2 * HEAD_DIM :] = out[:, 2 * HEAD_DIM :].astype(BF16)


def params(limit=None):
    return pltpu.CompilerParams(dimension_semantics=("arbitrary",), vmem_limit_bytes=limit)


def cost(flops, bytes_accessed, transcendentals=0):
    return pl.CostEstimate(
        flops=flops // 1000, transcendentals=0, bytes_accessed=bytes_accessed // 1000
    )


def project(rows, weight, bias, tables, block=512):
    count, width = rows.shape
    cols = bias.shape[1]
    table_spec = pl.BlockSpec((block, LANES), lambda i: (i, 0))
    return pl.pallas_call(
        project_kernel,
        grid=(count // block,),
        in_specs=[
            pl.BlockSpec((block, width), lambda i: (i, 0)),
            pl.BlockSpec((width, cols), lambda i: (0, 0)),
            pl.BlockSpec((1, cols), lambda i: (0, 0)),
            table_spec,
            table_spec,
            table_spec,
        ],
        out_specs=pl.BlockSpec((block, cols), lambda i: (i, 0)),
        out_shape=jax.ShapeDtypeStruct((count, cols), BF16),
        compiler_params=params(),
        cost_estimate=cost(2 * count * width * cols, 2 * (count * width + width * cols + count * cols)),
        name="project",
    )(rows, weight, bias, *tables)


def spread(column, width):
    return jnp.concatenate([column] * (width // LANES), axis=1)


def masked(scores, bias, block_idx, block):
    start = block_idx * block
    own = scores[start:]
    key_at = lax.broadcasted_iota(jnp.int32, own.shape, 0)
    query_at = lax.broadcasted_iota(jnp.int32, own.shape, 1)
    shift = spread(bias, block)
    own = jnp.where(
        key_at < query_at, own + shift[start:], jnp.where(key_at == query_at, own, masked_score)
    )
    if block_idx == 0:
        return own
    return jnp.concatenate([scores[:start] + shift[:start], own], axis=0)


def attend_kernel(query_ref, key_ref, value_ref, bias_ref, out_ref, total_ref, value_t, *, block):
    at = pl.program_id(0)

    @pl.when(at == 0)
    def _():
        value_t[...] = value_ref[...].T

    for block_idx in range(key_ref.shape[0] // block):

        @pl.when(at == block_idx)
        def _(block_idx=block_idx):
            end = (block_idx + 1) * block
            scores = masked(
                nt(key_ref[:end], query_ref[...]), bias_ref[:end], block_idx, block
            )
            top = jnp.max(scores, axis=0, keepdims=True)
            weights = jnp.exp(scores - top)
            total = jnp.sum(weights, axis=0, keepdims=True)
            out = nn(value_t[:, :end], weights.astype(BF16)) / total
            out_ref[...] = out.T.astype(BF16)
            total_ref[...] = jnp.broadcast_to(top + jnp.log(total), total_ref.shape)


def attend(qkv, bias, block=512):
    count = qkv.shape[0]
    pairs = count * (count + block) // 2
    return pl.pallas_call(
        partial(attend_kernel, block=block),
        grid=(count // block,),
        in_specs=[
            pl.BlockSpec((block, HEAD_DIM), lambda i: (i, 0)),
            pl.BlockSpec((count, HEAD_DIM), lambda i: (0, 1)),
            pl.BlockSpec((count, HEAD_DIM), lambda i: (0, 2)),
            pl.BlockSpec((count, LANES), lambda i: (0, 0)),
        ],
        out_specs=[
            pl.BlockSpec((block, HEAD_DIM), lambda i: (i, 0)),
            pl.BlockSpec((8, block), lambda i: (0, i)),
        ],
        out_shape=[
            jax.ShapeDtypeStruct((count, HEAD_DIM), BF16),
            jax.ShapeDtypeStruct((8, count), F32),
        ],
        scratch_shapes=[pltpu.VMEM((HEAD_DIM, count), BF16)],
        compiler_params=params(),
        cost_estimate=cost(4 * pairs * HEAD_DIM, 8 * count * HEAD_DIM, pairs),
        name="attend",
    )(qkv, qkv, qkv, bias)


def attend_back_kernel(
    query_ref, key_ref, value_ref, grad_ref, total_ref, bias_ref, cos_ref, sin_ref,
    out_ref, sums_ref, key_t, key_grad, value_grad, *, block
):
    at = pl.program_id(0)
    count = key_ref.shape[0]
    blocks = count // block

    @pl.when(at == 0)
    def _():
        key_t[...] = key_ref[...].T
        key_grad[...] = jnp.zeros_like(key_grad)
        value_grad[...] = jnp.zeros_like(value_grad)
        sums_ref[...] = jnp.zeros_like(sums_ref)

    for block_idx in range(blocks):

        @pl.when(at == block_idx)
        def _(block_idx=block_idx):
            start, end = block_idx * block, (block_idx + 1) * block
            query, grad = query_ref[...], grad_ref[...]
            scores = masked(nt(key_ref[:end], query), bias_ref[:end], block_idx, block)
            probs = jnp.exp(scores - total_ref[0:1])
            probs_grad = nt(value_ref[:end], grad)
            dots = jnp.sum(probs * probs_grad, axis=0, keepdims=True)
            score_grad = (probs * (probs_grad - dots)).astype(BF16)
            value_grad[:end] += nn(probs.astype(BF16), grad)
            key_grad[:end] += nn(score_grad, query)
            query_grad = nn(key_t[:, :end], score_grad) * (HEAD_DIM**-0.5)
            query_grad = rope_back_cols(
                query_grad, cos_ref[:, start:end], sin_ref[:, start:end]
            ).T.astype(BF16)
            out_ref[start:end, :HEAD_DIM] = query_grad
            sums_ref[:, :HEAD_DIM] += jnp.sum(query_grad.astype(F32), axis=0, keepdims=True)

    @pl.when(at == blocks - 1)
    def _():
        turned = rope_back_cols(key_grad[...].T, cos_ref[...], sin_ref[...]).T.astype(BF16)
        out_ref[:, HEAD_DIM : 2 * HEAD_DIM] = turned
        sums_ref[:, HEAD_DIM : 2 * HEAD_DIM] = jnp.sum(turned.astype(F32), axis=0, keepdims=True)
        low = value_grad[...].astype(BF16)
        out_ref[:, 2 * HEAD_DIM :] = low
        sums_ref[:, 2 * HEAD_DIM :] = jnp.sum(low.astype(F32), axis=0, keepdims=True)


def attend_back(qkv, grad, total, bias, cos_t, sin_t, block=512):
    count = qkv.shape[0]
    pairs = count * (count + block) // 2
    half = ROT // 2
    return pl.pallas_call(
        partial(attend_back_kernel, block=block),
        grid=(count // block,),
        in_specs=[
            pl.BlockSpec((block, HEAD_DIM), lambda i: (i, 0)),
            pl.BlockSpec((count, HEAD_DIM), lambda i: (0, 1)),
            pl.BlockSpec((count, HEAD_DIM), lambda i: (0, 2)),
            pl.BlockSpec((block, HEAD_DIM), lambda i: (i, 0)),
            pl.BlockSpec((8, block), lambda i: (0, i)),
            pl.BlockSpec((count, LANES), lambda i: (0, 0)),
            pl.BlockSpec((half, count), lambda i: (0, 0)),
            pl.BlockSpec((half, count), lambda i: (0, 0)),
        ],
        out_specs=[
            pl.BlockSpec((count, 3 * HEAD_DIM), lambda i: (0, 0)),
            pl.BlockSpec((1, 3 * HEAD_DIM), lambda i: (0, 0)),
        ],
        out_shape=[
            jax.ShapeDtypeStruct((count, 3 * HEAD_DIM), BF16),
            jax.ShapeDtypeStruct((1, 3 * HEAD_DIM), F32),
        ],
        scratch_shapes=[
            pltpu.VMEM((HEAD_DIM, count), BF16),
            pltpu.VMEM((count, HEAD_DIM), F32),
            pltpu.VMEM((count, HEAD_DIM), F32),
        ],
        compiler_params=params(),
        cost_estimate=cost(10 * pairs * HEAD_DIM, 16 * count * HEAD_DIM, pairs),
        name="attend_back",
    )(qkv, qkv, qkv, grad, total, bias, cos_t, sin_t)


def up_kernel(rows_ref, weight_ref, bias_ref, act_ref, slope_ref, *, chunk):
    rows = rows_ref[...]
    for at in range(0, weight_ref.shape[1], chunk):
        span = slice(at, at + chunk)
        hidden = nn(rows, weight_ref[:, span]) + bias_ref[:, span]
        share = 0.5 + 0.5 * lax.erf(hidden * 0.7071067811865476)
        density = jnp.exp(hidden * hidden * -0.5) * 0.3989422804014327
        act_ref[:, span] = (hidden * share).astype(BF16)
        slope_ref[:, span] = (share + hidden * density).astype(slope_ref.dtype)


def up_gelu(rows, weight, bias, block=256, chunk=256):
    count, width = rows.shape
    units = weight.shape[1]
    out_spec = pl.BlockSpec((block, units), lambda i: (i, 0))
    return pl.pallas_call(
        partial(up_kernel, chunk=chunk),
        grid=(count // block,),
        in_specs=[
            pl.BlockSpec((block, width), lambda i: (i, 0)),
            pl.BlockSpec((width, units), lambda i: (0, 0)),
            pl.BlockSpec((1, units), lambda i: (0, 0)),
        ],
        out_specs=[out_spec, out_spec],
        out_shape=[
            jax.ShapeDtypeStruct((count, units), BF16),
            jax.ShapeDtypeStruct((count, units), F32),
        ],
        compiler_params=params(),
        cost_estimate=cost(
            2 * count * width * units, 2 * (count * width + width * units + 3 * count * units), count * units
        ),
        name="up_gelu",
    )(rows, weight, bias)


def slope_kernel(grad_ref, weight_ref, slope_ref, out_ref, sums_ref, *, chunk):
    @pl.when(pl.program_id(0) == 0)
    def _():
        sums_ref[...] = jnp.zeros_like(sums_ref)

    grad = grad_ref[...]
    for at in range(0, weight_ref.shape[1], chunk):
        span = slice(at, at + chunk)
        low = (nn(grad, weight_ref[:, span]) * slope_ref[:, span]).astype(BF16)
        out_ref[:, span] = low
        sums_ref[:, span] += jnp.sum(low.astype(F32), axis=0, keepdims=True)


def hidden_back(grad, weight, slope, block=256, chunk=256):
    count, width = grad.shape
    units = weight.shape[1]
    return pl.pallas_call(
        partial(slope_kernel, chunk=chunk),
        grid=(count // block,),
        in_specs=[
            pl.BlockSpec((block, width), lambda i: (i, 0)),
            pl.BlockSpec((width, units), lambda i: (0, 0)),
            pl.BlockSpec((block, units), lambda i: (i, 0)),
        ],
        out_specs=[
            pl.BlockSpec((block, units), lambda i: (i, 0)),
            pl.BlockSpec((1, units), lambda i: (0, 0)),
        ],
        out_shape=[
            jax.ShapeDtypeStruct((count, units), BF16),
            jax.ShapeDtypeStruct((1, units), F32),
        ],
        compiler_params=params(),
        cost_estimate=cost(2 * count * width * units, 2 * (count * width + width * units + 3 * count * units)),
        name="hidden_back",
    )(grad, weight, slope)


def dgrad_sums(grad_ref, weight_ref, rows_ref, mean, inv, dot_ref, sum_ref, span):
    normed = nt(grad_ref[...], weight_ref[span])
    unit = (rows_ref[:, span].astype(F32) - mean) * inv
    dot_ref[:, span] += jnp.sum(normed * unit, axis=0, keepdims=True)
    sum_ref[:, span] += jnp.sum(normed, axis=0, keepdims=True)
    return normed


def dgrad_first_kernel(
    grad_ref, weight_ref, rows_ref, mean_ref, inv_ref, gain_ref, out_ref, dot_ref, sum_ref, *, chunk
):
    @pl.when(pl.program_id(0) == 0)
    def _():
        dot_ref[...] = jnp.zeros_like(dot_ref)
        sum_ref[...] = jnp.zeros_like(sum_ref)

    mean, inv = mean_ref[...], inv_ref[...]
    for at in range(0, weight_ref.shape[0], chunk):
        span = slice(at, at + chunk)
        normed = dgrad_sums(grad_ref, weight_ref, rows_ref, mean, inv, dot_ref, sum_ref, span)
        out_ref[:, span] = normed * gain_ref[:, span]


def dgrad_half_kernel(
    half_ref, grad_ref, weight_ref, rows_ref, mean_ref, inv_ref, gain_ref, before_ref,
    out_ref, dot_ref, sum_ref, *, chunk
):
    @pl.when(pl.program_id(0) == 0)
    def _():
        dot_ref[...] = jnp.zeros_like(dot_ref)
        sum_ref[...] = jnp.zeros_like(sum_ref)

    mean, inv = mean_ref[...], inv_ref[...]
    for at in range(0, weight_ref.shape[0], chunk):
        span = slice(at, at + chunk)
        normed = dgrad_sums(grad_ref, weight_ref, rows_ref, mean, inv, dot_ref, sum_ref, span)
        out_ref[:, span] = (normed * gain_ref[:, span] + before_ref[:, span]).astype(BF16)


def dgrad_first(grad, weight, rows, mean, inv, gain, block=256, chunk=256):
    count, width = rows.shape
    cols = grad.shape[1]
    wide = pl.BlockSpec((block, width), lambda i: (i, 0))
    thin = pl.BlockSpec((block, 1), lambda i: (i, 0))
    vector = pl.BlockSpec((1, width), lambda i: (0, 0))
    return pl.pallas_call(
        partial(dgrad_first_kernel, chunk=chunk),
        grid=(count // block,),
        in_specs=[
            pl.BlockSpec((block, cols), lambda i: (i, 0)),
            pl.BlockSpec((width, cols), lambda i: (0, 0)),
            wide,
            thin,
            thin,
            vector,
        ],
        out_specs=[wide, vector, vector],
        out_shape=[
            jax.ShapeDtypeStruct((count, width), F32),
            jax.ShapeDtypeStruct((1, width), F32),
            jax.ShapeDtypeStruct((1, width), F32),
        ],
        compiler_params=params(),
        cost_estimate=cost(2 * count * width * cols, 6 * count * width + 2 * width * cols),
        name="dgrad_first",
    )(grad, weight, rows, mean, inv, gain)


def dgrad_half(half, grad, weight, rows, mean, inv, gain, before, block=256, chunk=256):
    count, width = rows.shape
    cols = grad.shape[1]
    steps = count // block // 2
    wide = pl.BlockSpec((block, width), lambda i, h: (h[0] * steps + i, 0))
    thin = pl.BlockSpec((block, 1), lambda i, h: (h[0] * steps + i, 0))
    vector = pl.BlockSpec((1, width), lambda i, h: (0, 0))
    return pl.pallas_call(
        partial(dgrad_half_kernel, chunk=chunk),
        grid_spec=pltpu.PrefetchScalarGridSpec(
            num_scalar_prefetch=1,
            grid=(steps,),
            in_specs=[
                pl.BlockSpec((block, cols), lambda i, h: (h[0] * steps + i, 0)),
                pl.BlockSpec((width, cols), lambda i, h: (0, 0)),
                wide,
                thin,
                thin,
                vector,
                wide,
            ],
            out_specs=[pl.BlockSpec((block, width), lambda i, h: (i, 0)), vector, vector],
        ),
        out_shape=[
            jax.ShapeDtypeStruct((count // 2, width), BF16),
            jax.ShapeDtypeStruct((1, width), F32),
            jax.ShapeDtypeStruct((1, width), F32),
        ],
        compiler_params=params(),
        cost_estimate=cost(count * width * cols, 3 * count * width + 2 * width * cols),
        name="dgrad_half",
    )(half.reshape(1), grad, weight, rows, mean, inv, gain, before)


def branch_kernel(half_ref, heads_ref, out_ref_w, act_ref, down_ref, out_ref, *, chunk):
    heads, act = heads_ref[...], act_ref[...]
    for at in range(0, down_ref.shape[0], chunk):
        span = slice(at, at + chunk)
        out_ref[:, span] = (nt(heads, out_ref_w[span]) + nt(act, down_ref[span])).astype(BF16)


def branch_half(half, heads, pack, act, down, block=256, chunk=256):
    count = heads.shape[0]
    width, units = down.shape
    head_rows = heads.shape[1]
    last = pack.shape[1] // head_rows - 1
    steps = count // block // 2
    return pl.pallas_call(
        partial(branch_kernel, chunk=chunk),
        grid_spec=pltpu.PrefetchScalarGridSpec(
            num_scalar_prefetch=1,
            grid=(steps,),
            in_specs=[
                pl.BlockSpec((block, head_rows), lambda i, h: (h[0] * steps + i, 0)),
                pl.BlockSpec((width, head_rows), lambda i, h: (0, last)),
                pl.BlockSpec((block, units), lambda i, h: (h[0] * steps + i, 0)),
                pl.BlockSpec((width, units), lambda i, h: (0, 0)),
            ],
            out_specs=pl.BlockSpec((block, width), lambda i, h: (i, 0)),
        ),
        out_shape=jax.ShapeDtypeStruct((count // 2, width), BF16),
        compiler_params=params(),
        cost_estimate=cost(count * width * (units + head_rows), count * width + 2 * width * units + count * units),
        name="branch_half",
    )(half.reshape(1), heads, pack, act, down)


def weight_grad_kernel(*refs, pairs):
    out_ref = refs[-1]
    at = 0
    for pair in range(pairs):
        rows_ref, cols_ref = refs[2 * pair], refs[2 * pair + 1]
        span = slice(at, at + cols_ref.shape[1])
        out_ref[:, span] = lax.dot_general(
            rows_ref[...], cols_ref[...], (((0,), (0,)), ((), ())), preferred_element_type=F32
        ).astype(BF16)
        at += cols_ref.shape[1]


def weight_grad(pairs, count):
    width = pairs[0][0].shape[1]
    block = width // (2 * count)
    total = sum(cols.shape[1] for _, cols in pairs)
    tokens = pairs[0][0].shape[0]
    if block % LANES:
        grads = [
            jnp.einsum("rd,rc->dc", rows, cols, preferred_element_type=F32) for rows, cols in pairs
        ]
        grads = jnp.concatenate(grads, axis=1).astype(BF16).reshape(2, count, block, total)
        return grads.transpose(1, 0, 2, 3).reshape(width, total)
    specs = []
    for rows, cols in pairs:
        specs.append(pl.BlockSpec((tokens, block), lambda i: (0, (i % 2) * count + i // 2)))
        specs.append(pl.BlockSpec(cols.shape, lambda i: (0, 0)))
    return pl.pallas_call(
        partial(weight_grad_kernel, pairs=len(pairs)),
        grid=(2 * count,),
        in_specs=specs,
        out_specs=pl.BlockSpec((block, total), lambda i: (i, 0)),
        out_shape=jax.ShapeDtypeStruct((width, total), BF16),
        compiler_params=params(),
        cost_estimate=cost(2 * tokens * width * total, 2 * (tokens * (width + total) + width * total)),
        name="weight_grad",
    )(*[array for pair in pairs for array in pair])


def place_kernel(core_ref, rows_ref, *refs):
    refs[-1][...] = rows_ref[...]


def place_half(half, rows, before=None, block=256):
    count, width = rows.shape
    steps = count // block
    operands, specs = [rows], [pl.BlockSpec((block, width), lambda i, h: (i, 0))]
    if before is not None:
        operands.append(before)
        specs.append(pl.BlockSpec(memory_space=pl.ANY))
    return pl.pallas_call(
        place_kernel,
        grid_spec=pltpu.PrefetchScalarGridSpec(
            num_scalar_prefetch=1,
            grid=(steps,),
            in_specs=specs,
            out_specs=pl.BlockSpec((block, width), lambda i, h: (h[0] * steps + i, 0)),
        ),
        out_shape=jax.ShapeDtypeStruct((2 * count, width), rows.dtype),
        input_output_aliases={} if before is None else {2: 0},
        compiler_params=params(),
        cost_estimate=cost(0, 4 * count * width),
        name="place_half",
    )(half.reshape(1), *operands)


CORE = [(0, 1), (1, 0), (2, 3), (3, 2)]
YAX = [(0, 2), (2, 0), (1, 3), (3, 1)]
XAX = [(0, 1), (1, 0)]


def core_swap(block):
    return lax.ppermute(block, "tensor", CORE)


def y_swap(block):
    return lax.ppermute(block, "tensor", YAX)


def x_swap(block):
    return lax.ppermute(block, "branch", XAX)


def pick(array, index, size, axis=0):
    return lax.dynamic_slice_in_dim(array, index * size, size, axis)


def add16(first, second):
    return (first.astype(F32) + second.astype(F32)).astype(BF16)


def own_rows(array, core, why, ex):
    rows = array.shape[0]
    sixteenth = rows // 16
    first = core * 8 + why * 2 + ex
    second = core * 8 + 4 + ex * 2 + why
    return pick(array, first, sixteenth), pick(array, second, sixteenth)


def join(low_index, mine, other, axis=0):
    return jnp.where(
        low_index == 0,
        jnp.concatenate([mine, other], axis),
        jnp.concatenate([other, mine], axis),
    )


def after(value, *first):
    return lax.optimization_barrier((value,) + first)[0]


def rows_at(array, start, index, size):
    return lax.dynamic_slice_in_dim(array, start + index * size, size, 0)


def halving_send(keep, got, why, ex):
    quarter = keep.shape[0] // 2
    eighth = quarter // 2

    def send(start, index):
        return add16(rows_at(keep, start, index, eighth), rows_at(got, start, index, eighth))

    return send(0, 1 - why), send(quarter, 1 - ex)


def halving_more(keep, got, two, why, ex):
    quarter = keep.shape[0] // 2
    eighth, sixteenth = quarter // 2, quarter // 4

    def mine(start, index, received, part):
        at = start + index * eighth
        return (
            rows_at(keep, at, part, sixteenth).astype(F32)
            + rows_at(got, at, part, sixteenth).astype(F32)
            + rows_at(received, 0, part, sixteenth).astype(F32)
        )

    kept = mine(0, why, two[0], ex), mine(quarter, ex, two[1], why)
    sent = (
        mine(0, why, two[0], 1 - ex).astype(BF16),
        mine(quarter, ex, two[1], 1 - why).astype(BF16),
    )
    return kept, sent


def gather_one(first, second):
    return x_swap(first), y_swap(second)


def gather_two(first, second, got, why, ex):
    first, second = join(ex, first, got[0]), join(why, second, got[1])
    return (first, second), (y_swap(first), x_swap(second))


def gather_last(two, got, core, why, ex):
    first, second = join(why, two[0], got[0]), join(ex, two[1], got[1])
    mine = jnp.concatenate([first, second], 0)
    return mine, core_swap(mine)


def local(
    tokens,
    lengths,
    valid_mask,
    ln1_gain,
    ln1_bias,
    qkv_weight,
    qkv_bias,
    out_weight,
    out_bias,
    ln2_gain,
    ln2_bias,
    up_weight,
    up_bias,
    down_weight,
    down_bias,
    out_grad,
    *,
    count,
):
    row_count, width = tokens.shape
    ex = lax.axis_index("branch")
    tensor_at = lax.axis_index("tensor")
    why, core = tensor_at // 2, tensor_at % 2
    place = lax.axis_index("dp")
    qkv_cols = qkv_bias.shape[0] // 2
    head_rows = out_weight.shape[0] // 2
    units = up_bias.shape[0] // 2
    chunk = width // (2 * count)

    heads_shard = jnp.concatenate(
        [pick(qkv_weight, ex, qkv_cols, 1), pick(out_weight, ex, head_rows, 0).T], axis=1
    )
    up_shard = pick(up_weight, ex, units, 1)
    down_shard = pick(down_weight, ex, units, 0).T
    heads_full = lax.all_gather(heads_shard, "dp", axis=0, tiled=True)
    up_full = lax.all_gather(up_shard, "dp", axis=0, tiled=True)
    down_full = lax.all_gather(down_shard, "dp", axis=0, tiled=True)

    positions = jnp.arange(row_count, dtype=jnp.int32)
    seq_valid = (valid_mask == 1) & (positions < lengths[0])
    validity = seq_valid.astype(F32)
    key_bias = jnp.broadcast_to(
        jnp.where(seq_valid, 0.0, masked_score)[:, None], (row_count, LANES)
    )
    rows_f32 = tokens.astype(F32)
    mean = jnp.mean(rows_f32, axis=-1, keepdims=True)
    centred = rows_f32 - mean
    inv_std = lax.rsqrt(jnp.mean(centred * centred, axis=-1, keepdims=True) + norm_eps)
    unit_rows = centred * inv_std
    grad_rows = out_grad * validity.astype(BF16)[:, None]
    normed1 = (unit_rows * ln1_gain + ln1_bias).astype(BF16)
    normed2 = (unit_rows * ln2_gain + ln2_bias).astype(BF16)
    cos_table, sin_table = rope_tables(row_count, ROT)
    gap = jnp.zeros((row_count, ROT // 2), F32)
    rest = jnp.zeros((row_count, LANES - ROT), F32)
    tables = (
        jnp.concatenate([cos_table, cos_table, rest + 1.0], axis=1),
        jnp.concatenate([-sin_table, gap, rest], axis=1),
        jnp.concatenate([gap, sin_table, rest], axis=1),
    )

    qkv = project(normed1, heads_full, pick(qkv_bias, ex, qkv_cols)[None], tables)
    attended, log_total = attend(qkv, key_bias)
    attended_grad = jnp.dot(
        grad_rows, heads_full[:, qkv_cols:], preferred_element_type=F32
    ).astype(BF16)
    qkv_grad, qkv_bias_part = attend_back(
        qkv, attended_grad, log_total, key_bias, cos_table.T, sin_table.T
    )
    heads_partial = weight_grad([(normed1, qkv_grad), (grad_rows, attended)], count)

    def scatter(partial_sum):
        return lax.psum_scatter(partial_sum, "dp", scatter_dimension=0, tiled=True)

    heads_total = scatter(heads_partial)
    input_part, dot1, sum1 = dgrad_first(
        after(qkv_grad, heads_partial), heads_full, tokens, mean, inv_std, ln1_gain[None]
    )
    activated, slope = up_gelu(
        after(normed2, input_part), up_full, pick(up_bias, ex, units)[None]
    )
    down_partial = weight_grad([(after(grad_rows, activated), activated)], count)
    down_total = scatter(down_partial)

    shift_sum = out_bias + down_bias
    tokens_own = own_rows(tokens, core, why, ex)
    validity_own = own_rows(validity, core, why, ex)
    out_grad_own = own_rows(out_grad, core, why, ex)
    mean_own = own_rows(mean, core, why, ex)
    inv_own = own_rows(inv_std, core, why, ex)

    def output_of(at, total):
        return (
            tokens_own[at].astype(F32) + validity_own[at][:, None] * (total + shift_sum)
        ).astype(BF16)

    def input_of(at, total):
        unit = (tokens_own[at].astype(F32) - mean_own[at]) * inv_own[at]
        back = inv_own[at] * (
            total
            - jnp.mean(total, axis=-1, keepdims=True)
            - unit * jnp.mean(total * unit, axis=-1, keepdims=True)
        )
        return (out_grad_own[at].astype(F32) + back).astype(BF16)

    branch_send = branch_half(
        1 - core, attended, heads_full, after(activated, down_partial), down_full
    )
    branch_core = core_swap(branch_send)
    branch_keep = branch_half(core, attended, heads_full, after(activated, branch_send), down_full)
    branch_core = after(branch_core, branch_keep)
    branch_two = halving_send(branch_keep, branch_core, why, ex)
    branch_two_got = y_swap(branch_two[0]), x_swap(branch_two[1])
    hidden_grad, up_bias_part = hidden_back(
        after(grad_rows, branch_keep, *branch_two), down_full, slope
    )
    norm_rows = tokens, mean, inv_std, ln2_gain[None], input_part
    branch_two_got = after(branch_two_got, hidden_grad)
    branch_mine, branch_three = halving_more(branch_keep, branch_core, branch_two_got, why, ex)
    branch_three_got = x_swap(branch_three[0]), y_swap(branch_three[1])
    input_send, dot2, sum2 = dgrad_half(
        1 - core, after(hidden_grad, *branch_three), up_full, *norm_rows
    )
    input_core = core_swap(input_send)
    input_keep, dot3, sum3 = dgrad_half(core, after(hidden_grad, input_send), up_full, *norm_rows)
    input_core = after(input_core, input_keep)
    input_two = halving_send(input_keep, input_core, why, ex)
    input_two_got = y_swap(input_two[0]), x_swap(input_two[1])
    branch_three_got = after(branch_three_got, *input_two)
    output_one = [
        output_of(at, branch_mine[at] + branch_three_got[at].astype(F32)) for at in range(2)
    ]
    output_got = gather_one(*output_one)
    dot2, sum2 = dot2 + dot3, sum2 + sum3
    vectors = jnp.concatenate(
        [
            dot1[0],
            sum1[0],
            dot2[0],
            sum2[0],
            jnp.sum(grad_rows, axis=0, dtype=F32),
            qkv_bias_part[0],
            up_bias_part[0],
        ]
    ).reshape(-1, LANES)
    hops = [
        lax.ppermute(vectors, "dp", [(k, (k + hop) % count) for k in range(count)])
        for hop in range(1, count)
    ]
    up_partial = weight_grad([(after(normed2, vectors, *output_one), hidden_grad)], count)
    up_total = scatter(up_partial)
    hops = after(hops, up_partial)
    vectors = sum(hops, vectors)
    norm_count, bias_rows = 4 * width // LANES, width // LANES
    norms, bias_grad, biases = (
        vectors[:norm_count],
        vectors[norm_count : norm_count + bias_rows].reshape(width),
        vectors[norm_count + bias_rows :],
    )

    def share(total):
        mine, given = pick(total, ex, chunk), pick(total, 1 - ex, chunk)
        return mine.astype(F32), x_swap(given.astype(BF16))

    heads_mine, heads_other = share(after(heads_total, up_partial))
    norms_other, biases_other = core_swap(norms), x_swap(biases)
    input_two_got = after(input_two_got, up_partial, norms)
    input_mine, input_three = halving_more(input_keep, input_core, input_two_got, why, ex)
    input_three_got = x_swap(input_three[0]), y_swap(input_three[1])
    output_got, norms_other, biases_other, heads_other = after(
        (output_got, norms_other, biases_other, heads_other), *input_three
    )
    output_two, output_got = gather_two(*output_one, output_got, why, ex)
    norms = norms + norms_other
    norms_other = y_swap(norms)
    input_three_got, norms_other = after(
        (input_three_got, norms_other), norms, *output_two
    )
    input_one = [input_of(at, input_mine[at] + input_three_got[at].astype(F32)) for at in range(2)]
    input_got = gather_one(*input_one)
    norms = norms + norms_other
    norms_other = x_swap(norms)
    output_got, norms_other, down_total = after(
        (output_got, norms_other, down_total), norms, *input_one
    )
    output_mine, output_other = gather_last(output_two, output_got, core, why, ex)
    down_mine, down_other = share(down_total)
    input_got = after(input_got, output_mine)
    input_two, input_got = gather_two(*input_one, input_got, why, ex)
    norms = (norms + norms_other).reshape(4, width)
    biases, other = biases.reshape(-1), biases_other.reshape(-1)
    qkv_bias_grad = join(ex, biases[:qkv_cols], other[:qkv_cols])
    up_bias_grad = join(ex, biases[qkv_cols:], other[qkv_cols:])
    other = heads_other.astype(F32)
    qkv_out = join(ex, heads_mine[:, :qkv_cols], other[:, :qkv_cols], 1)
    out_out = join(ex, heads_mine[:, qkv_cols:].T, other[:, qkv_cols:].T, 0)
    down_out = join(ex, down_mine.T, down_other.T.astype(F32), 0)
    output_rows = place_half(
        1 - core, output_other, place_half(core, after(output_mine, *input_two))
    )
    input_got = after(input_got, output_rows, norms, qkv_out, out_out, down_out)
    input_mine, input_other = gather_last(input_two, input_got, core, why, ex)
    up_mine, up_other = share(after(up_total, input_mine))
    grad_half = place_half(core, input_mine)
    up_out = join(ex, up_mine, up_other.astype(F32), 1)
    grad_input = place_half(1 - core, after(input_other, up_out), grad_half)

    return (
        output_rows,
        grad_input,
        norms[0],
        norms[1],
        qkv_out,
        qkv_bias_grad,
        out_out,
        bias_grad,
        norms[2],
        norms[3],
        up_out,
        up_bias_grad,
        down_out,
        bias_grad,
    )


def solution(mesh):
    return jax.shard_map(
        partial(local, count=mesh.shape["dp"]),
        mesh=mesh,
        in_specs=(
            P("dp", None),
            P("dp"),
            P("dp"),
            P(),
            P(),
            P("dp", "tensor"),
            P("tensor"),
            P("tensor", "dp"),
            P(),
            P(),
            P(),
            P("dp", "tensor"),
            P("tensor"),
            P("tensor", "dp"),
            P(),
            P("dp", None),
        ),
        out_specs=(
            P("dp", None),
            P("dp", None),
            P(),
            P(),
            P(("branch", "dp"), "tensor"),
            P("tensor"),
            P("tensor", ("branch", "dp")),
            P(),
            P(),
            P(),
            P(("branch", "dp"), "tensor"),
            P("tensor"),
            P("tensor", ("branch", "dp")),
            P(),
        ),
        check_vma=False,
    )
```

```python
from functools import partial

import jax
import jax.numpy as jnp
from jax import lax
from jax.experimental import pallas as pl
from jax.experimental.pallas import tpu as pltpu
from jax.sharding import PartitionSpec as P

HEAD_DIM = 256
SEQ_LEN = 2048
ROT = 64
LANES = 128
BF16 = jnp.bfloat16
F32 = jnp.float32

norm_eps = 1e-05
rope_base = 10000.0
masked_score = -1e30


def rope_tables(length, rotary):
    half_rot = rotary // 2
    inv_freq = rope_base ** (-2.0 * jnp.arange(half_rot, dtype=F32) / rotary)
    phase_angle = jnp.arange(length, dtype=F32)[:, None] * inv_freq[None, :]
    return (jnp.cos(phase_angle), jnp.sin(phase_angle))


def rope_back_cols(grad, cos_t, sin_t):
    half = ROT // 2
    lead, tail = grad[:half], grad[half:ROT]
    return jnp.concatenate(
        [lead * cos_t + tail * sin_t, tail * cos_t - lead * sin_t, grad[ROT:]], axis=0
    )


def nn(first, second):
    return lax.dot_general(first, second, (((1,), (0,)), ((), ())), preferred_element_type=F32)


def nt(first, second):
    return lax.dot_general(first, second, (((1,), (1,)), ((), ())), preferred_element_type=F32)


def project_kernel(rows_ref, weight_ref, bias_ref, cos_ref, ahead_ref, behind_ref, out_ref):
    out = nn(rows_ref[...], weight_ref[...]) + bias_ref[...]
    half = ROT // 2
    for part in range(2):
        base = part * HEAD_DIM
        lead = out[:, base : base + LANES]
        turned = (
            lead * cos_ref[...]
            + pltpu.roll(lead, LANES - half, 1) * ahead_ref[...]
            + pltpu.roll(lead, half, 1) * behind_ref[...]
        )
        scale = HEAD_DIM**-0.5 if part == 0 else 1.0
        out_ref[:, base : base + LANES] = (turned * scale).astype(BF16)
        rest = out[:, base + LANES : base + HEAD_DIM]
        out_ref[:, base + LANES : base + HEAD_DIM] = (rest * scale).astype(BF16)
    out_ref[:, 2 * HEAD_DIM :] = out[:, 2 * HEAD_DIM :].astype(BF16)


def params(limit=None):
    return pltpu.CompilerParams(dimension_semantics=("arbitrary",), vmem_limit_bytes=limit)


def cost(flops, bytes_accessed, transcendentals=0):
    return pl.CostEstimate(
        flops=flops // 1000, transcendentals=0, bytes_accessed=bytes_accessed // 1000
    )


def project(rows, weight, bias, tables, block=512):
    count, width = rows.shape
    cols = bias.shape[1]
    table_spec = pl.BlockSpec((block, LANES), lambda i: (i, 0))
    return pl.pallas_call(
        project_kernel,
        grid=(count // block,),
        in_specs=[
            pl.BlockSpec((block, width), lambda i: (i, 0)),
            pl.BlockSpec((width, cols), lambda i: (0, 0)),
            pl.BlockSpec((1, cols), lambda i: (0, 0)),
            table_spec,
            table_spec,
            table_spec,
        ],
        out_specs=pl.BlockSpec((block, cols), lambda i: (i, 0)),
        out_shape=jax.ShapeDtypeStruct((count, cols), BF16),
        compiler_params=params(),
        cost_estimate=cost(2 * count * width * cols, 2 * (count * width + width * cols + count * cols)),
        name="project",
    )(rows, weight, bias, *tables)


def spread(column, width):
    return jnp.concatenate([column] * (width // LANES), axis=1)


def masked(scores, bias, block_idx, block):
    start = block_idx * block
    own = scores[start:]
    key_at = lax.broadcasted_iota(jnp.int32, own.shape, 0)
    query_at = lax.broadcasted_iota(jnp.int32, own.shape, 1)
    shift = spread(bias, block)
    own = jnp.where(
        key_at < query_at, own + shift[start:], jnp.where(key_at == query_at, own, masked_score)
    )
    if block_idx == 0:
        return own
    return jnp.concatenate([scores[:start] + shift[:start], own], axis=0)


def attend_kernel(query_ref, key_ref, value_ref, bias_ref, out_ref, total_ref, value_t, *, block):
    at = pl.program_id(0)

    @pl.when(at == 0)
    def _():
        value_t[...] = value_ref[...].T

    for block_idx in range(key_ref.shape[0] // block):

        @pl.when(at == block_idx)
        def _(block_idx=block_idx):
            end = (block_idx + 1) * block
            scores = masked(
                nt(key_ref[:end], query_ref[...]), bias_ref[:end], block_idx, block
            )
            top = jnp.max(scores, axis=0, keepdims=True)
            weights = jnp.exp(scores - top)
            total = jnp.sum(weights, axis=0, keepdims=True)
            out = nn(value_t[:, :end], weights.astype(BF16)) / total
            out_ref[...] = out.T.astype(BF16)
            total_ref[...] = jnp.broadcast_to(top + jnp.log(total), total_ref.shape)


def attend(qkv, bias, block=512):
    count = qkv.shape[0]
    pairs = count * (count + block) // 2
    return pl.pallas_call(
        partial(attend_kernel, block=block),
        grid=(count // block,),
        in_specs=[
            pl.BlockSpec((block, HEAD_DIM), lambda i: (i, 0)),
            pl.BlockSpec((count, HEAD_DIM), lambda i: (0, 1)),
            pl.BlockSpec((count, HEAD_DIM), lambda i: (0, 2)),
            pl.BlockSpec((count, LANES), lambda i: (0, 0)),
        ],
        out_specs=[
            pl.BlockSpec((block, HEAD_DIM), lambda i: (i, 0)),
            pl.BlockSpec((8, block), lambda i: (0, i)),
        ],
        out_shape=[
            jax.ShapeDtypeStruct((count, HEAD_DIM), BF16),
            jax.ShapeDtypeStruct((8, count), F32),
        ],
        scratch_shapes=[pltpu.VMEM((HEAD_DIM, count), BF16)],
        compiler_params=params(),
        cost_estimate=cost(4 * pairs * HEAD_DIM, 8 * count * HEAD_DIM, pairs),
        name="attend",
    )(qkv, qkv, qkv, bias)


def attend_back_kernel(
    query_ref, key_ref, value_ref, grad_ref, total_ref, bias_ref, cos_ref, sin_ref,
    out_ref, sums_ref, key_t, key_grad, value_grad, *, block
):
    at = pl.program_id(0)
    count = key_ref.shape[0]
    blocks = count // block

    @pl.when(at == 0)
    def _():
        key_t[...] = key_ref[...].T
        key_grad[...] = jnp.zeros_like(key_grad)
        value_grad[...] = jnp.zeros_like(value_grad)
        sums_ref[...] = jnp.zeros_like(sums_ref)

    for block_idx in range(blocks):

        @pl.when(at == block_idx)
        def _(block_idx=block_idx):
            start, end = block_idx * block, (block_idx + 1) * block
            query, grad = query_ref[...], grad_ref[...]
            scores = masked(nt(key_ref[:end], query), bias_ref[:end], block_idx, block)
            probs = jnp.exp(scores - total_ref[0:1])
            probs_grad = nt(value_ref[:end], grad)
            dots = jnp.sum(probs * probs_grad, axis=0, keepdims=True)
            score_grad = (probs * (probs_grad - dots)).astype(BF16)
            value_grad[:end] += nn(probs.astype(BF16), grad)
            key_grad[:end] += nn(score_grad, query)
            query_grad = nn(key_t[:, :end], score_grad) * (HEAD_DIM**-0.5)
            query_grad = rope_back_cols(
                query_grad, cos_ref[:, start:end], sin_ref[:, start:end]
            ).T.astype(BF16)
            out_ref[start:end, :HEAD_DIM] = query_grad
            sums_ref[:, :HEAD_DIM] += jnp.sum(query_grad.astype(F32), axis=0, keepdims=True)

    @pl.when(at == blocks - 1)
    def _():
        turned = rope_back_cols(key_grad[...].T, cos_ref[...], sin_ref[...]).T.astype(BF16)
        out_ref[:, HEAD_DIM : 2 * HEAD_DIM] = turned
        sums_ref[:, HEAD_DIM : 2 * HEAD_DIM] = jnp.sum(turned.astype(F32), axis=0, keepdims=True)
        low = value_grad[...].astype(BF16)
        out_ref[:, 2 * HEAD_DIM :] = low
        sums_ref[:, 2 * HEAD_DIM :] = jnp.sum(low.astype(F32), axis=0, keepdims=True)


def attend_back(qkv, grad, total, bias, cos_t, sin_t, block=512):
    count = qkv.shape[0]
    pairs = count * (count + block) // 2
    half = ROT // 2
    return pl.pallas_call(
        partial(attend_back_kernel, block=block),
        grid=(count // block,),
        in_specs=[
            pl.BlockSpec((block, HEAD_DIM), lambda i: (i, 0)),
            pl.BlockSpec((count, HEAD_DIM), lambda i: (0, 1)),
            pl.BlockSpec((count, HEAD_DIM), lambda i: (0, 2)),
            pl.BlockSpec((block, HEAD_DIM), lambda i: (i, 0)),
            pl.BlockSpec((8, block), lambda i: (0, i)),
            pl.BlockSpec((count, LANES), lambda i: (0, 0)),
            pl.BlockSpec((half, count), lambda i: (0, 0)),
            pl.BlockSpec((half, count), lambda i: (0, 0)),
        ],
        out_specs=[
            pl.BlockSpec((count, 3 * HEAD_DIM), lambda i: (0, 0)),
            pl.BlockSpec((1, 3 * HEAD_DIM), lambda i: (0, 0)),
        ],
        out_shape=[
            jax.ShapeDtypeStruct((count, 3 * HEAD_DIM), BF16),
            jax.ShapeDtypeStruct((1, 3 * HEAD_DIM), F32),
        ],
        scratch_shapes=[
            pltpu.VMEM((HEAD_DIM, count), BF16),
            pltpu.VMEM((count, HEAD_DIM), F32),
            pltpu.VMEM((count, HEAD_DIM), F32),
        ],
        compiler_params=params(),
        cost_estimate=cost(10 * pairs * HEAD_DIM, 16 * count * HEAD_DIM, pairs),
        name="attend_back",
    )(qkv, qkv, qkv, grad, total, bias, cos_t, sin_t)


def up_kernel(rows_ref, weight_ref, bias_ref, act_ref, slope_ref, *, chunk):
    rows = rows_ref[...]
    for at in range(0, weight_ref.shape[1], chunk):
        span = slice(at, at + chunk)
        hidden = nn(rows, weight_ref[:, span]) + bias_ref[:, span]
        share = 0.5 + 0.5 * lax.erf(hidden * 0.7071067811865476)
        density = jnp.exp(hidden * hidden * -0.5) * 0.3989422804014327
        act_ref[:, span] = (hidden * share).astype(BF16)
        slope_ref[:, span] = (share + hidden * density).astype(slope_ref.dtype)


def up_gelu(rows, weight, bias, block=256, chunk=256):
    count, width = rows.shape
    units = weight.shape[1]
    out_spec = pl.BlockSpec((block, units), lambda i: (i, 0))
    return pl.pallas_call(
        partial(up_kernel, chunk=chunk),
        grid=(count // block,),
        in_specs=[
            pl.BlockSpec((block, width), lambda i: (i, 0)),
            pl.BlockSpec((width, units), lambda i: (0, 0)),
            pl.BlockSpec((1, units), lambda i: (0, 0)),
        ],
        out_specs=[out_spec, out_spec],
        out_shape=[
            jax.ShapeDtypeStruct((count, units), BF16),
            jax.ShapeDtypeStruct((count, units), F32),
        ],
        compiler_params=params(),
        cost_estimate=cost(
            2 * count * width * units, 2 * (count * width + width * units + 3 * count * units), count * units
        ),
        name="up_gelu",
    )(rows, weight, bias)


def slope_kernel(grad_ref, weight_ref, slope_ref, out_ref, sums_ref, *, chunk):
    @pl.when(pl.program_id(0) == 0)
    def _():
        sums_ref[...] = jnp.zeros_like(sums_ref)

    grad = grad_ref[...]
    for at in range(0, weight_ref.shape[1], chunk):
        span = slice(at, at + chunk)
        low = (nn(grad, weight_ref[:, span]) * slope_ref[:, span]).astype(BF16)
        out_ref[:, span] = low
        sums_ref[:, span] += jnp.sum(low.astype(F32), axis=0, keepdims=True)


def hidden_back(grad, weight, slope, block=256, chunk=256):
    count, width = grad.shape
    units = weight.shape[1]
    return pl.pallas_call(
        partial(slope_kernel, chunk=chunk),
        grid=(count // block,),
        in_specs=[
            pl.BlockSpec((block, width), lambda i: (i, 0)),
            pl.BlockSpec((width, units), lambda i: (0, 0)),
            pl.BlockSpec((block, units), lambda i: (i, 0)),
        ],
        out_specs=[
            pl.BlockSpec((block, units), lambda i: (i, 0)),
            pl.BlockSpec((1, units), lambda i: (0, 0)),
        ],
        out_shape=[
            jax.ShapeDtypeStruct((count, units), BF16),
            jax.ShapeDtypeStruct((1, units), F32),
        ],
        compiler_params=params(),
        cost_estimate=cost(2 * count * width * units, 2 * (count * width + width * units + 3 * count * units)),
        name="hidden_back",
    )(grad, weight, slope)


def dgrad_sums(grad_ref, weight_ref, rows_ref, mean, inv, dot_ref, sum_ref, span):
    normed = nt(grad_ref[...], weight_ref[span])
    unit = (rows_ref[:, span].astype(F32) - mean) * inv
    dot_ref[:, span] += jnp.sum(normed * unit, axis=0, keepdims=True)
    sum_ref[:, span] += jnp.sum(normed, axis=0, keepdims=True)
    return normed


def dgrad_first_kernel(
    grad_ref, weight_ref, rows_ref, mean_ref, inv_ref, gain_ref, out_ref, dot_ref, sum_ref, *, chunk
):
    @pl.when(pl.program_id(0) == 0)
    def _():
        dot_ref[...] = jnp.zeros_like(dot_ref)
        sum_ref[...] = jnp.zeros_like(sum_ref)

    mean, inv = mean_ref[...], inv_ref[...]
    for at in range(0, weight_ref.shape[0], chunk):
        span = slice(at, at + chunk)
        normed = dgrad_sums(grad_ref, weight_ref, rows_ref, mean, inv, dot_ref, sum_ref, span)
        out_ref[:, span] = normed * gain_ref[:, span]


def dgrad_half_kernel(
    half_ref, grad_ref, weight_ref, rows_ref, mean_ref, inv_ref, gain_ref, before_ref,
    out_ref, dot_ref, sum_ref, *, chunk
):
    @pl.when(pl.program_id(0) == 0)
    def _():
        dot_ref[...] = jnp.zeros_like(dot_ref)
        sum_ref[...] = jnp.zeros_like(sum_ref)

    mean, inv = mean_ref[...], inv_ref[...]
    for at in range(0, weight_ref.shape[0], chunk):
        span = slice(at, at + chunk)
        normed = dgrad_sums(grad_ref, weight_ref, rows_ref, mean, inv, dot_ref, sum_ref, span)
        out_ref[:, span] = (normed * gain_ref[:, span] + before_ref[:, span]).astype(BF16)


def dgrad_first(grad, weight, rows, mean, inv, gain, block=256, chunk=256):
    count, width = rows.shape
    cols = grad.shape[1]
    wide = pl.BlockSpec((block, width), lambda i: (i, 0))
    thin = pl.BlockSpec((block, 1), lambda i: (i, 0))
    vector = pl.BlockSpec((1, width), lambda i: (0, 0))
    return pl.pallas_call(
        partial(dgrad_first_kernel, chunk=chunk),
        grid=(count // block,),
        in_specs=[
            pl.BlockSpec((block, cols), lambda i: (i, 0)),
            pl.BlockSpec((width, cols), lambda i: (0, 0)),
            wide,
            thin,
            thin,
            vector,
        ],
        out_specs=[wide, vector, vector],
        out_shape=[
            jax.ShapeDtypeStruct((count, width), F32),
            jax.ShapeDtypeStruct((1, width), F32),
            jax.ShapeDtypeStruct((1, width), F32),
        ],
        compiler_params=params(),
        cost_estimate=cost(2 * count * width * cols, 6 * count * width + 2 * width * cols),
        name="dgrad_first",
    )(grad, weight, rows, mean, inv, gain)


def dgrad_half(half, grad, weight, rows, mean, inv, gain, before, block=256, chunk=256):
    count, width = rows.shape
    cols = grad.shape[1]
    steps = count // block // 2
    wide = pl.BlockSpec((block, width), lambda i, h: (h[0] * steps + i, 0))
    thin = pl.BlockSpec((block, 1), lambda i, h: (h[0] * steps + i, 0))
    vector = pl.BlockSpec((1, width), lambda i, h: (0, 0))
    return pl.pallas_call(
        partial(dgrad_half_kernel, chunk=chunk),
        grid_spec=pltpu.PrefetchScalarGridSpec(
            num_scalar_prefetch=1,
            grid=(steps,),
            in_specs=[
                pl.BlockSpec((block, cols), lambda i, h: (h[0] * steps + i, 0)),
                pl.BlockSpec((width, cols), lambda i, h: (0, 0)),
                wide,
                thin,
                thin,
                vector,
                wide,
            ],
            out_specs=[pl.BlockSpec((block, width), lambda i, h: (i, 0)), vector, vector],
        ),
        out_shape=[
            jax.ShapeDtypeStruct((count // 2, width), BF16),
            jax.ShapeDtypeStruct((1, width), F32),
            jax.ShapeDtypeStruct((1, width), F32),
        ],
        compiler_params=params(),
        cost_estimate=cost(count * width * cols, 3 * count * width + 2 * width * cols),
        name="dgrad_half",
    )(half.reshape(1), grad, weight, rows, mean, inv, gain, before)


def branch_kernel(half_ref, heads_ref, out_ref_w, act_ref, down_ref, out_ref, *, chunk):
    heads, act = heads_ref[...], act_ref[...]
    for at in range(0, down_ref.shape[0], chunk):
        span = slice(at, at + chunk)
        out_ref[:, span] = (nt(heads, out_ref_w[span]) + nt(act, down_ref[span])).astype(BF16)


def branch_half(half, heads, pack, act, down, block=256, chunk=256):
    count = heads.shape[0]
    width, units = down.shape
    head_rows = heads.shape[1]
    last = pack.shape[1] // head_rows - 1
    steps = count // block // 2
    return pl.pallas_call(
        partial(branch_kernel, chunk=chunk),
        grid_spec=pltpu.PrefetchScalarGridSpec(
            num_scalar_prefetch=1,
            grid=(steps,),
            in_specs=[
                pl.BlockSpec((block, head_rows), lambda i, h: (h[0] * steps + i, 0)),
                pl.BlockSpec((width, head_rows), lambda i, h: (0, last)),
                pl.BlockSpec((block, units), lambda i, h: (h[0] * steps + i, 0)),
                pl.BlockSpec((width, units), lambda i, h: (0, 0)),
            ],
            out_specs=pl.BlockSpec((block, width), lambda i, h: (i, 0)),
        ),
        out_shape=jax.ShapeDtypeStruct((count // 2, width), BF16),
        compiler_params=params(),
        cost_estimate=cost(count * width * (units + head_rows), count * width + 2 * width * units + count * units),
        name="branch_half",
    )(half.reshape(1), heads, pack, act, down)


def weight_grad_kernel(*refs, pairs):
    out_ref = refs[-1]
    at = 0
    for pair in range(pairs):
        rows_ref, cols_ref = refs[2 * pair], refs[2 * pair + 1]
        span = slice(at, at + cols_ref.shape[1])
        out_ref[:, span] = lax.dot_general(
            rows_ref[...], cols_ref[...], (((0,), (0,)), ((), ())), preferred_element_type=F32
        ).astype(BF16)
        at += cols_ref.shape[1]


def weight_grad(pairs, count):
    width = pairs[0][0].shape[1]
    block = width // (2 * count)
    total = sum(cols.shape[1] for _, cols in pairs)
    tokens = pairs[0][0].shape[0]
    if block % LANES:
        grads = [
            jnp.einsum("rd,rc->dc", rows, cols, preferred_element_type=F32) for rows, cols in pairs
        ]
        grads = jnp.concatenate(grads, axis=1).astype(BF16).reshape(2, count, block, total)
        return grads.transpose(1, 0, 2, 3).reshape(width, total)
    specs = []
    for rows, cols in pairs:
        specs.append(pl.BlockSpec((tokens, block), lambda i: (0, (i % 2) * count + i // 2)))
        specs.append(pl.BlockSpec(cols.shape, lambda i: (0, 0)))
    return pl.pallas_call(
        partial(weight_grad_kernel, pairs=len(pairs)),
        grid=(2 * count,),
        in_specs=specs,
        out_specs=pl.BlockSpec((block, total), lambda i: (i, 0)),
        out_shape=jax.ShapeDtypeStruct((width, total), BF16),
        compiler_params=params(),
        cost_estimate=cost(2 * tokens * width * total, 2 * (tokens * (width + total) + width * total)),
        name="weight_grad",
    )(*[array for pair in pairs for array in pair])


def place_kernel(core_ref, rows_ref, *refs):
    refs[-1][...] = rows_ref[...]


def place_half(half, rows, before=None, block=256):
    count, width = rows.shape
    steps = count // block
    operands, specs = [rows], [pl.BlockSpec((block, width), lambda i, h: (i, 0))]
    if before is not None:
        operands.append(before)
        specs.append(pl.BlockSpec(memory_space=pl.ANY))
    return pl.pallas_call(
        place_kernel,
        grid_spec=pltpu.PrefetchScalarGridSpec(
            num_scalar_prefetch=1,
            grid=(steps,),
            in_specs=specs,
            out_specs=pl.BlockSpec((block, width), lambda i, h: (h[0] * steps + i, 0)),
        ),
        out_shape=jax.ShapeDtypeStruct((2 * count, width), rows.dtype),
        input_output_aliases={} if before is None else {2: 0},
        compiler_params=params(),
        cost_estimate=cost(0, 4 * count * width),
        name="place_half",
    )(half.reshape(1), *operands)


CORE = [(0, 1), (1, 0), (2, 3), (3, 2)]
YAX = [(0, 2), (2, 0), (1, 3), (3, 1)]
XAX = [(0, 1), (1, 0)]


def core_swap(block):
    return lax.ppermute(block, "tensor", CORE)


def y_swap(block):
    return lax.ppermute(block, "tensor", YAX)


def x_swap(block):
    return lax.ppermute(block, "branch", XAX)


def pick(array, index, size, axis=0):
    return lax.dynamic_slice_in_dim(array, index * size, size, axis)


def add16(first, second):
    return (first.astype(F32) + second.astype(F32)).astype(BF16)


def own_rows(array, core, why, ex):
    rows = array.shape[0]
    sixteenth = rows // 16
    first = core * 8 + why * 2 + ex
    second = core * 8 + 4 + ex * 2 + why
    return pick(array, first, sixteenth), pick(array, second, sixteenth)


def join(low_index, mine, other, axis=0):
    return jnp.where(
        low_index == 0,
        jnp.concatenate([mine, other], axis),
        jnp.concatenate([other, mine], axis),
    )


def after(value, *first):
    return lax.optimization_barrier((value,) + first)[0]


def rows_at(array, start, index, size):
    return lax.dynamic_slice_in_dim(array, start + index * size, size, 0)


def halving_send(keep, got, why, ex):
    quarter = keep.shape[0] // 2
    eighth = quarter // 2

    def send(start, index):
        return add16(rows_at(keep, start, index, eighth), rows_at(got, start, index, eighth))

    return send(0, 1 - why), send(quarter, 1 - ex)


def halving_more(keep, got, two, why, ex):
    quarter = keep.shape[0] // 2
    eighth, sixteenth = quarter // 2, quarter // 4

    def mine(start, index, received, part):
        at = start + index * eighth
        return (
            rows_at(keep, at, part, sixteenth).astype(F32)
            + rows_at(got, at, part, sixteenth).astype(F32)
            + rows_at(received, 0, part, sixteenth).astype(F32)
        )

    kept = mine(0, why, two[0], ex), mine(quarter, ex, two[1], why)
    sent = (
        mine(0, why, two[0], 1 - ex).astype(BF16),
        mine(quarter, ex, two[1], 1 - why).astype(BF16),
    )
    return kept, sent


def gather_one(first, second):
    return x_swap(first), y_swap(second)


def gather_two(first, second, got, why, ex):
    first, second = join(ex, first, got[0]), join(why, second, got[1])
    return (first, second), (y_swap(first), x_swap(second))


def gather_last(two, got, core, why, ex):
    first, second = join(why, two[0], got[0]), join(ex, two[1], got[1])
    mine = jnp.concatenate([first, second], 0)
    return mine, core_swap(mine)


def local(
    tokens,
    lengths,
    valid_mask,
    ln1_gain,
    ln1_bias,
    qkv_weight,
    qkv_bias,
    out_weight,
    out_bias,
    ln2_gain,
    ln2_bias,
    up_weight,
    up_bias,
    down_weight,
    down_bias,
    out_grad,
    *,
    count,
):
    row_count, width = tokens.shape
    ex = lax.axis_index("branch")
    tensor_at = lax.axis_index("tensor")
    why, core = tensor_at // 2, tensor_at % 2
    place = lax.axis_index("dp")
    qkv_cols = qkv_bias.shape[0] // 2
    head_rows = out_weight.shape[0] // 2
    units = up_bias.shape[0] // 2
    chunk = width // (2 * count)

    heads_shard = jnp.concatenate(
        [pick(qkv_weight, ex, qkv_cols, 1), pick(out_weight, ex, head_rows, 0).T], axis=1
    )
    up_shard = pick(up_weight, ex, units, 1)
    down_shard = pick(down_weight, ex, units, 0).T
    heads_full = lax.all_gather(heads_shard, "dp", axis=0, tiled=True)
    up_full = lax.all_gather(up_shard, "dp", axis=0, tiled=True)
    down_full = lax.all_gather(down_shard, "dp", axis=0, tiled=True)

    positions = jnp.arange(row_count, dtype=jnp.int32)
    seq_valid = (valid_mask == 1) & (positions < lengths[0])
    validity = seq_valid.astype(F32)
    key_bias = jnp.broadcast_to(
        jnp.where(seq_valid, 0.0, masked_score)[:, None], (row_count, LANES)
    )
    rows_f32 = tokens.astype(F32)
    mean = jnp.mean(rows_f32, axis=-1, keepdims=True)
    centred = rows_f32 - mean
    inv_std = lax.rsqrt(jnp.mean(centred * centred, axis=-1, keepdims=True) + norm_eps)
    unit_rows = centred * inv_std
    grad_rows = out_grad * validity.astype(BF16)[:, None]
    normed1 = (unit_rows * ln1_gain + ln1_bias).astype(BF16)
    normed2 = (unit_rows * ln2_gain + ln2_bias).astype(BF16)
    cos_table, sin_table = rope_tables(row_count, ROT)
    gap = jnp.zeros((row_count, ROT // 2), F32)
    rest = jnp.zeros((row_count, LANES - ROT), F32)
    tables = (
        jnp.concatenate([cos_table, cos_table, rest + 1.0], axis=1),
        jnp.concatenate([-sin_table, gap, rest], axis=1),
        jnp.concatenate([gap, sin_table, rest], axis=1),
    )

    qkv = project(normed1, heads_full, pick(qkv_bias, ex, qkv_cols)[None], tables)
    attended, log_total = attend(qkv, key_bias)
    attended_grad = jnp.dot(
        grad_rows, heads_full[:, qkv_cols:], preferred_element_type=F32
    ).astype(BF16)
    qkv_grad, qkv_bias_part = attend_back(
        qkv, attended_grad, log_total, key_bias, cos_table.T, sin_table.T
    )
    def scatter(partial_sum):
        return lax.psum_scatter(partial_sum, "dp", scatter_dimension=0, tiled=True)

    input_part, dot1, sum1 = dgrad_first(
        qkv_grad, heads_full, tokens, mean, inv_std, ln1_gain[None]
    )
    activated, slope = up_gelu(
        after(normed2, input_part), up_full, pick(up_bias, ex, units)[None]
    )
    down_partial = weight_grad(
        [
            (normed1, after(qkv_grad, activated)),
            (grad_rows, attended),
            (after(grad_rows, activated), activated),
        ],
        count,
    )
    first_total = scatter(down_partial)

    shift_sum = out_bias + down_bias
    tokens_own = own_rows(tokens, core, why, ex)
    validity_own = own_rows(validity, core, why, ex)
    out_grad_own = own_rows(out_grad, core, why, ex)
    mean_own = own_rows(mean, core, why, ex)
    inv_own = own_rows(inv_std, core, why, ex)

    def output_of(at, total):
        return (
            tokens_own[at].astype(F32) + validity_own[at][:, None] * (total + shift_sum)
        ).astype(BF16)

    def input_of(at, total):
        unit = (tokens_own[at].astype(F32) - mean_own[at]) * inv_own[at]
        back = inv_own[at] * (
            total
            - jnp.mean(total, axis=-1, keepdims=True)
            - unit * jnp.mean(total * unit, axis=-1, keepdims=True)
        )
        return (out_grad_own[at].astype(F32) + back).astype(BF16)

    branch_send = branch_half(
        1 - core, attended, heads_full, after(activated, down_partial), down_full
    )
    branch_core = core_swap(branch_send)
    branch_keep = branch_half(core, attended, heads_full, after(activated, branch_send), down_full)
    branch_core = after(branch_core, branch_keep)
    branch_two = halving_send(branch_keep, branch_core, why, ex)
    branch_two_got = y_swap(branch_two[0]), x_swap(branch_two[1])
    hidden_grad, up_bias_part = hidden_back(
        after(grad_rows, branch_keep, *branch_two), down_full, slope
    )
    norm_rows = tokens, mean, inv_std, ln2_gain[None], input_part
    branch_two_got = after(branch_two_got, hidden_grad)
    branch_mine, branch_three = halving_more(branch_keep, branch_core, branch_two_got, why, ex)
    branch_three_got = x_swap(branch_three[0]), y_swap(branch_three[1])
    input_send, dot2, sum2 = dgrad_half(
        1 - core, after(hidden_grad, *branch_three), up_full, *norm_rows
    )
    input_core = core_swap(input_send)
    input_keep, dot3, sum3 = dgrad_half(core, after(hidden_grad, input_send), up_full, *norm_rows)
    input_core = after(input_core, input_keep)
    input_two = halving_send(input_keep, input_core, why, ex)
    input_two_got = y_swap(input_two[0]), x_swap(input_two[1])
    branch_three_got = after(branch_three_got, *input_two)
    output_one = [
        output_of(at, branch_mine[at] + branch_three_got[at].astype(F32)) for at in range(2)
    ]
    output_got = gather_one(*output_one)
    dot2, sum2 = dot2 + dot3, sum2 + sum3
    vectors = jnp.concatenate(
        [
            dot1[0],
            sum1[0],
            dot2[0],
            sum2[0],
            jnp.sum(grad_rows, axis=0, dtype=F32),
            qkv_bias_part[0],
            up_bias_part[0],
        ]
    ).reshape(-1, LANES)
    hops = [
        lax.ppermute(vectors, "dp", [(k, (k + hop) % count) for k in range(count)])
        for hop in range(1, count)
    ]
    up_partial = weight_grad([(after(normed2, vectors, *output_one), hidden_grad)], count)
    up_total = scatter(up_partial)
    input_two_got = after(input_two_got, up_partial)
    input_mine, input_three = halving_more(input_keep, input_core, input_two_got, why, ex)
    input_three_got = x_swap(input_three[0]), y_swap(input_three[1])
    output_got, hops = after((output_got, hops), *input_three)
    output_two, output_got = gather_two(*output_one, output_got, why, ex)
    vectors = sum(after(hops, *output_two), vectors)
    norm_count, bias_rows = 4 * width // LANES, width // LANES
    norms, bias_grad, biases = (
        vectors[:norm_count],
        vectors[norm_count : norm_count + bias_rows].reshape(width),
        vectors[norm_count + bias_rows :],
    )
    norms_other, biases_other = core_swap(norms), x_swap(biases)
    input_three_got = after(input_three_got, norms, *output_two)
    input_one = [input_of(at, input_mine[at] + input_three_got[at].astype(F32)) for at in range(2)]
    input_got = gather_one(*input_one)
    norms, biases_other = after((norms + norms_other, biases_other), *input_one)
    norms_other = y_swap(norms)
    output_got = after(output_got, norms, *input_one)
    output_mine, output_other = gather_last(output_two, output_got, core, why, ex)
    input_got, norms_other = after((input_got, norms_other), output_mine)
    norms = norms + norms_other
    norms_other = x_swap(norms)
    input_got = after(input_got, norms)
    input_two, input_got = gather_two(*input_one, input_got, why, ex)
    def halves(total):
        return pick(total, ex, chunk).astype(F32), pick(total, 1 - ex, chunk)

    def share(total):
        mine, given = halves(total)
        return mine, x_swap(given)

    first_mine, first_other = share(after(first_total, *input_two))
    output_half = place_half(core, after(output_mine, *input_two))
    output_rows = place_half(1 - core, after(output_other, output_half), output_half)
    biases, other = biases.reshape(-1), biases_other.reshape(-1)
    qkv_bias_grad = join(ex, biases[:qkv_cols], other[:qkv_cols])
    up_bias_grad = join(ex, biases[qkv_cols:], other[qkv_cols:])
    input_got, norms_other = after((input_got, norms_other), output_rows)
    norms = (norms + norms_other).reshape(4, width)
    input_mine, input_other = gather_last(input_two, input_got, core, why, ex)
    up_mine, up_given = halves(after(up_total, input_mine))
    up_other = x_swap(up_given)
    first_other = after(first_other, up_given)
    heads_mine, down_mine = first_mine[:, :-units], first_mine[:, -units:]
    other, down_other = first_other[:, :-units].astype(F32), first_other[:, -units:].astype(F32)
    qkv_out = join(ex, heads_mine[:, :qkv_cols], other[:, :qkv_cols], 1)
    out_out = join(ex, heads_mine[:, qkv_cols:].T, other[:, qkv_cols:].T, 0)
    down_out = join(ex, down_mine.T, down_other.T, 0)
    grad_half = place_half(core, after(input_mine, norms, up_given))
    grad_input = place_half(1 - core, after(input_other, grad_half), grad_half)
    up_other = after(up_other, qkv_out, out_out, down_out, grad_input)
    up_out = join(ex, up_mine, up_other.astype(F32), 1)

    return (
        output_rows,
        grad_input,
        norms[0],
        norms[1],
        qkv_out,
        qkv_bias_grad,
        out_out,
        bias_grad,
        norms[2],
        norms[3],
        up_out,
        up_bias_grad,
        down_out,
        bias_grad,
    )


def solution(mesh):
    return jax.shard_map(
        partial(local, count=mesh.shape["dp"]),
        mesh=mesh,
        in_specs=(
            P("dp", None),
            P("dp"),
            P("dp"),
            P(),
            P(),
            P("dp", "tensor"),
            P("tensor"),
            P("tensor", "dp"),
            P(),
            P(),
            P(),
            P("dp", "tensor"),
            P("tensor"),
            P("tensor", "dp"),
            P(),
            P("dp", None),
        ),
        out_specs=(
            P("dp", None),
            P("dp", None),
            P(),
            P(),
            P(("branch", "dp"), "tensor"),
            P("tensor"),
            P("tensor", ("branch", "dp")),
            P(),
            P(),
            P(),
            P(("branch", "dp"), "tensor"),
            P("tensor"),
            P("tensor", ("branch", "dp")),
            P(),
        ),
        check_vma=False,
    )
```

```python
from functools import partial

import jax
import jax.numpy as jnp
from jax import lax
from jax.experimental import pallas as pl
from jax.experimental.pallas import tpu as pltpu
from jax.sharding import PartitionSpec as P

HEAD_DIM = 256
SEQ_LEN = 2048
ROT = 64
LANES = 128
BF16 = jnp.bfloat16
F32 = jnp.float32

norm_eps = 1e-05
rope_base = 10000.0
masked_score = -1e30


def rope_tables(length, rotary):
    half_rot = rotary // 2
    inv_freq = rope_base ** (-2.0 * jnp.arange(half_rot, dtype=F32) / rotary)
    phase_angle = jnp.arange(length, dtype=F32)[:, None] * inv_freq[None, :]
    return (jnp.cos(phase_angle), jnp.sin(phase_angle))


def rope_back_cols(grad, cos_t, sin_t):
    half = ROT // 2
    lead, tail = grad[:half], grad[half:ROT]
    return jnp.concatenate(
        [lead * cos_t + tail * sin_t, tail * cos_t - lead * sin_t, grad[ROT:]], axis=0
    )


def nn(first, second):
    return lax.dot_general(first, second, (((1,), (0,)), ((), ())), preferred_element_type=F32)


def nt(first, second):
    return lax.dot_general(first, second, (((1,), (1,)), ((), ())), preferred_element_type=F32)


def project_kernel(rows_ref, weight_ref, bias_ref, cos_ref, ahead_ref, behind_ref, out_ref):
    out = nn(rows_ref[...], weight_ref[...]) + bias_ref[...]
    half = ROT // 2
    for part in range(2):
        base = part * HEAD_DIM
        lead = out[:, base : base + LANES]
        turned = (
            lead * cos_ref[...]
            + pltpu.roll(lead, LANES - half, 1) * ahead_ref[...]
            + pltpu.roll(lead, half, 1) * behind_ref[...]
        )
        scale = HEAD_DIM**-0.5 if part == 0 else 1.0
        out_ref[:, base : base + LANES] = (turned * scale).astype(BF16)
        rest = out[:, base + LANES : base + HEAD_DIM]
        out_ref[:, base + LANES : base + HEAD_DIM] = (rest * scale).astype(BF16)
    out_ref[:, 2 * HEAD_DIM :] = out[:, 2 * HEAD_DIM :].astype(BF16)


def params(limit=None):
    return pltpu.CompilerParams(dimension_semantics=("arbitrary",), vmem_limit_bytes=limit)


def cost(flops, bytes_accessed, transcendentals=0):
    return pl.CostEstimate(
        flops=flops // 1000, transcendentals=0, bytes_accessed=bytes_accessed // 1000
    )


def project(rows, weight, bias, tables, block=512):
    count, width = rows.shape
    cols = bias.shape[1]
    table_spec = pl.BlockSpec((block, LANES), lambda i: (i, 0))
    return pl.pallas_call(
        project_kernel,
        grid=(count // block,),
        in_specs=[
            pl.BlockSpec((block, width), lambda i: (i, 0)),
            pl.BlockSpec((width, cols), lambda i: (0, 0)),
            pl.BlockSpec((1, cols), lambda i: (0, 0)),
            table_spec,
            table_spec,
            table_spec,
        ],
        out_specs=pl.BlockSpec((block, cols), lambda i: (i, 0)),
        out_shape=jax.ShapeDtypeStruct((count, cols), BF16),
        compiler_params=params(),
        cost_estimate=cost(2 * count * width * cols, 2 * (count * width + width * cols + count * cols)),
        name="project",
    )(rows, weight, bias, *tables)


def spread(column, width):
    return jnp.concatenate([column] * (width // LANES), axis=1)


def masked(scores, bias, block_idx, block):
    start = block_idx * block
    own = scores[start:]
    key_at = lax.broadcasted_iota(jnp.int32, own.shape, 0)
    query_at = lax.broadcasted_iota(jnp.int32, own.shape, 1)
    shift = spread(bias, block)
    own = jnp.where(
        key_at < query_at, own + shift[start:], jnp.where(key_at == query_at, own, masked_score)
    )
    if block_idx == 0:
        return own
    return jnp.concatenate([scores[:start] + shift[:start], own], axis=0)


def attend_kernel(query_ref, key_ref, value_ref, bias_ref, out_ref, total_ref, value_t, *, block):
    at = pl.program_id(0)

    @pl.when(at == 0)
    def _():
        value_t[...] = value_ref[...].T

    for block_idx in range(key_ref.shape[0] // block):

        @pl.when(at == block_idx)
        def _(block_idx=block_idx):
            end = (block_idx + 1) * block
            scores = masked(
                nt(key_ref[:end], query_ref[...]), bias_ref[:end], block_idx, block
            )
            top = jnp.max(scores, axis=0, keepdims=True)
            weights = jnp.exp(scores - top)
            total = jnp.sum(weights, axis=0, keepdims=True)
            out = nn(value_t[:, :end], weights.astype(BF16)) / total
            out_ref[...] = out.T.astype(BF16)
            total_ref[...] = jnp.broadcast_to(top + jnp.log(total), total_ref.shape)


def attend(qkv, bias, block=512):
    count = qkv.shape[0]
    pairs = count * (count + block) // 2
    return pl.pallas_call(
        partial(attend_kernel, block=block),
        grid=(count // block,),
        in_specs=[
            pl.BlockSpec((block, HEAD_DIM), lambda i: (i, 0)),
            pl.BlockSpec((count, HEAD_DIM), lambda i: (0, 1)),
            pl.BlockSpec((count, HEAD_DIM), lambda i: (0, 2)),
            pl.BlockSpec((count, LANES), lambda i: (0, 0)),
        ],
        out_specs=[
            pl.BlockSpec((block, HEAD_DIM), lambda i: (i, 0)),
            pl.BlockSpec((8, block), lambda i: (0, i)),
        ],
        out_shape=[
            jax.ShapeDtypeStruct((count, HEAD_DIM), BF16),
            jax.ShapeDtypeStruct((8, count), F32),
        ],
        scratch_shapes=[pltpu.VMEM((HEAD_DIM, count), BF16)],
        compiler_params=params(),
        cost_estimate=cost(4 * pairs * HEAD_DIM, 8 * count * HEAD_DIM, pairs),
        name="attend",
    )(qkv, qkv, qkv, bias)


def attend_back_kernel(
    query_ref, key_ref, value_ref, grad_ref, total_ref, bias_ref, cos_ref, sin_ref,
    out_ref, sums_ref, key_t, key_grad, value_grad, *, block
):
    at = pl.program_id(0)
    count = key_ref.shape[0]
    blocks = count // block

    @pl.when(at == 0)
    def _():
        key_t[...] = key_ref[...].T
        key_grad[...] = jnp.zeros_like(key_grad)
        value_grad[...] = jnp.zeros_like(value_grad)
        sums_ref[...] = jnp.zeros_like(sums_ref)

    for block_idx in range(blocks):

        @pl.when(at == block_idx)
        def _(block_idx=block_idx):
            start, end = block_idx * block, (block_idx + 1) * block
            query, grad = query_ref[...], grad_ref[...]
            scores = masked(nt(key_ref[:end], query), bias_ref[:end], block_idx, block)
            probs = jnp.exp(scores - total_ref[0:1])
            probs_grad = nt(value_ref[:end], grad)
            dots = jnp.sum(probs * probs_grad, axis=0, keepdims=True)
            score_grad = (probs * (probs_grad - dots)).astype(BF16)
            value_grad[:end] += nn(probs.astype(BF16), grad)
            key_grad[:end] += nn(score_grad, query)
            query_grad = nn(key_t[:, :end], score_grad) * (HEAD_DIM**-0.5)
            query_grad = rope_back_cols(
                query_grad, cos_ref[:, start:end], sin_ref[:, start:end]
            ).T.astype(BF16)
            out_ref[start:end, :HEAD_DIM] = query_grad
            sums_ref[:, :HEAD_DIM] += jnp.sum(query_grad.astype(F32), axis=0, keepdims=True)

    @pl.when(at == blocks - 1)
    def _():
        turned = rope_back_cols(key_grad[...].T, cos_ref[...], sin_ref[...]).T.astype(BF16)
        out_ref[:, HEAD_DIM : 2 * HEAD_DIM] = turned
        sums_ref[:, HEAD_DIM : 2 * HEAD_DIM] = jnp.sum(turned.astype(F32), axis=0, keepdims=True)
        low = value_grad[...].astype(BF16)
        out_ref[:, 2 * HEAD_DIM :] = low
        sums_ref[:, 2 * HEAD_DIM :] = jnp.sum(low.astype(F32), axis=0, keepdims=True)


def attend_back(qkv, grad, total, bias, cos_t, sin_t, block=512):
    count = qkv.shape[0]
    pairs = count * (count + block) // 2
    half = ROT // 2
    return pl.pallas_call(
        partial(attend_back_kernel, block=block),
        grid=(count // block,),
        in_specs=[
            pl.BlockSpec((block, HEAD_DIM), lambda i: (i, 0)),
            pl.BlockSpec((count, HEAD_DIM), lambda i: (0, 1)),
            pl.BlockSpec((count, HEAD_DIM), lambda i: (0, 2)),
            pl.BlockSpec((block, HEAD_DIM), lambda i: (i, 0)),
            pl.BlockSpec((8, block), lambda i: (0, i)),
            pl.BlockSpec((count, LANES), lambda i: (0, 0)),
            pl.BlockSpec((half, count), lambda i: (0, 0)),
            pl.BlockSpec((half, count), lambda i: (0, 0)),
        ],
        out_specs=[
            pl.BlockSpec((count, 3 * HEAD_DIM), lambda i: (0, 0)),
            pl.BlockSpec((1, 3 * HEAD_DIM), lambda i: (0, 0)),
        ],
        out_shape=[
            jax.ShapeDtypeStruct((count, 3 * HEAD_DIM), BF16),
            jax.ShapeDtypeStruct((1, 3 * HEAD_DIM), F32),
        ],
        scratch_shapes=[
            pltpu.VMEM((HEAD_DIM, count), BF16),
            pltpu.VMEM((count, HEAD_DIM), F32),
            pltpu.VMEM((count, HEAD_DIM), F32),
        ],
        compiler_params=params(),
        cost_estimate=cost(10 * pairs * HEAD_DIM, 16 * count * HEAD_DIM, pairs),
        name="attend_back",
    )(qkv, qkv, qkv, grad, total, bias, cos_t, sin_t)


def up_kernel(rows_ref, weight_ref, bias_ref, act_ref, slope_ref, *, chunk):
    rows = rows_ref[...]
    for at in range(0, weight_ref.shape[1], chunk):
        span = slice(at, at + chunk)
        hidden = nn(rows, weight_ref[:, span]) + bias_ref[:, span]
        share = 0.5 + 0.5 * lax.erf(hidden * 0.7071067811865476)
        density = jnp.exp(hidden * hidden * -0.5) * 0.3989422804014327
        act_ref[:, span] = (hidden * share).astype(BF16)
        slope_ref[:, span] = (share + hidden * density).astype(slope_ref.dtype)


def up_gelu(rows, weight, bias, block=256, chunk=256):
    count, width = rows.shape
    units = weight.shape[1]
    out_spec = pl.BlockSpec((block, units), lambda i: (i, 0))
    return pl.pallas_call(
        partial(up_kernel, chunk=chunk),
        grid=(count // block,),
        in_specs=[
            pl.BlockSpec((block, width), lambda i: (i, 0)),
            pl.BlockSpec((width, units), lambda i: (0, 0)),
            pl.BlockSpec((1, units), lambda i: (0, 0)),
        ],
        out_specs=[out_spec, out_spec],
        out_shape=[
            jax.ShapeDtypeStruct((count, units), BF16),
            jax.ShapeDtypeStruct((count, units), F32),
        ],
        compiler_params=params(),
        cost_estimate=cost(
            2 * count * width * units, 2 * (count * width + width * units + 3 * count * units), count * units
        ),
        name="up_gelu",
    )(rows, weight, bias)


def slope_kernel(grad_ref, weight_ref, slope_ref, out_ref, sums_ref, *, chunk):
    @pl.when(pl.program_id(0) == 0)
    def _():
        sums_ref[...] = jnp.zeros_like(sums_ref)

    grad = grad_ref[...]
    for at in range(0, weight_ref.shape[1], chunk):
        span = slice(at, at + chunk)
        low = (nn(grad, weight_ref[:, span]) * slope_ref[:, span]).astype(BF16)
        out_ref[:, span] = low
        sums_ref[:, span] += jnp.sum(low.astype(F32), axis=0, keepdims=True)


def hidden_back(grad, weight, slope, block=256, chunk=256):
    count, width = grad.shape
    units = weight.shape[1]
    return pl.pallas_call(
        partial(slope_kernel, chunk=chunk),
        grid=(count // block,),
        in_specs=[
            pl.BlockSpec((block, width), lambda i: (i, 0)),
            pl.BlockSpec((width, units), lambda i: (0, 0)),
            pl.BlockSpec((block, units), lambda i: (i, 0)),
        ],
        out_specs=[
            pl.BlockSpec((block, units), lambda i: (i, 0)),
            pl.BlockSpec((1, units), lambda i: (0, 0)),
        ],
        out_shape=[
            jax.ShapeDtypeStruct((count, units), BF16),
            jax.ShapeDtypeStruct((1, units), F32),
        ],
        compiler_params=params(),
        cost_estimate=cost(2 * count * width * units, 2 * (count * width + width * units + 3 * count * units)),
        name="hidden_back",
    )(grad, weight, slope)


def dgrad_sums(grad_ref, weight_ref, rows_ref, mean, inv, dot_ref, sum_ref, span):
    normed = nt(grad_ref[...], weight_ref[span])
    unit = (rows_ref[:, span].astype(F32) - mean) * inv
    dot_ref[:, span] += jnp.sum(normed * unit, axis=0, keepdims=True)
    sum_ref[:, span] += jnp.sum(normed, axis=0, keepdims=True)
    return normed


def dgrad_first_kernel(
    grad_ref, weight_ref, rows_ref, mean_ref, inv_ref, gain_ref, out_ref, dot_ref, sum_ref, *, chunk
):
    @pl.when(pl.program_id(0) == 0)
    def _():
        dot_ref[...] = jnp.zeros_like(dot_ref)
        sum_ref[...] = jnp.zeros_like(sum_ref)

    mean, inv = mean_ref[...], inv_ref[...]
    for at in range(0, weight_ref.shape[0], chunk):
        span = slice(at, at + chunk)
        normed = dgrad_sums(grad_ref, weight_ref, rows_ref, mean, inv, dot_ref, sum_ref, span)
        out_ref[:, span] = normed * gain_ref[:, span]


def dgrad_half_kernel(
    half_ref, grad_ref, weight_ref, rows_ref, mean_ref, inv_ref, gain_ref, before_ref,
    out_ref, dot_ref, sum_ref, *, chunk
):
    @pl.when(pl.program_id(0) == 0)
    def _():
        dot_ref[...] = jnp.zeros_like(dot_ref)
        sum_ref[...] = jnp.zeros_like(sum_ref)

    mean, inv = mean_ref[...], inv_ref[...]
    for at in range(0, weight_ref.shape[0], chunk):
        span = slice(at, at + chunk)
        normed = dgrad_sums(grad_ref, weight_ref, rows_ref, mean, inv, dot_ref, sum_ref, span)
        out_ref[:, span] = (normed * gain_ref[:, span] + before_ref[:, span]).astype(BF16)


def dgrad_first(grad, weight, rows, mean, inv, gain, block=256, chunk=256):
    count, width = rows.shape
    cols = grad.shape[1]
    wide = pl.BlockSpec((block, width), lambda i: (i, 0))
    thin = pl.BlockSpec((block, 1), lambda i: (i, 0))
    vector = pl.BlockSpec((1, width), lambda i: (0, 0))
    return pl.pallas_call(
        partial(dgrad_first_kernel, chunk=chunk),
        grid=(count // block,),
        in_specs=[
            pl.BlockSpec((block, cols), lambda i: (i, 0)),
            pl.BlockSpec((width, cols), lambda i: (0, 0)),
            wide,
            thin,
            thin,
            vector,
        ],
        out_specs=[wide, vector, vector],
        out_shape=[
            jax.ShapeDtypeStruct((count, width), F32),
            jax.ShapeDtypeStruct((1, width), F32),
            jax.ShapeDtypeStruct((1, width), F32),
        ],
        compiler_params=params(),
        cost_estimate=cost(2 * count * width * cols, 6 * count * width + 2 * width * cols),
        name="dgrad_first",
    )(grad, weight, rows, mean, inv, gain)


def dgrad_half(half, grad, weight, rows, mean, inv, gain, before, block=256, chunk=256):
    count, width = rows.shape
    cols = grad.shape[1]
    steps = count // block // 2
    wide = pl.BlockSpec((block, width), lambda i, h: (h[0] * steps + i, 0))
    thin = pl.BlockSpec((block, 1), lambda i, h: (h[0] * steps + i, 0))
    vector = pl.BlockSpec((1, width), lambda i, h: (0, 0))
    return pl.pallas_call(
        partial(dgrad_half_kernel, chunk=chunk),
        grid_spec=pltpu.PrefetchScalarGridSpec(
            num_scalar_prefetch=1,
            grid=(steps,),
            in_specs=[
                pl.BlockSpec((block, cols), lambda i, h: (h[0] * steps + i, 0)),
                pl.BlockSpec((width, cols), lambda i, h: (0, 0)),
                wide,
                thin,
                thin,
                vector,
                wide,
            ],
            out_specs=[pl.BlockSpec((block, width), lambda i, h: (i, 0)), vector, vector],
        ),
        out_shape=[
            jax.ShapeDtypeStruct((count // 2, width), BF16),
            jax.ShapeDtypeStruct((1, width), F32),
            jax.ShapeDtypeStruct((1, width), F32),
        ],
        compiler_params=params(),
        cost_estimate=cost(count * width * cols, 3 * count * width + 2 * width * cols),
        name="dgrad_half",
    )(half.reshape(1), grad, weight, rows, mean, inv, gain, before)


def branch_kernel(half_ref, heads_ref, out_ref_w, act_ref, down_ref, out_ref, *, chunk):
    heads, act = heads_ref[...], act_ref[...]
    for at in range(0, down_ref.shape[0], chunk):
        span = slice(at, at + chunk)
        out_ref[:, span] = (nt(heads, out_ref_w[span]) + nt(act, down_ref[span])).astype(BF16)


def branch_half(half, heads, pack, act, down, block=256, chunk=256):
    count = heads.shape[0]
    width, units = down.shape
    head_rows = heads.shape[1]
    last = pack.shape[1] // head_rows - 1
    steps = count // block // 2
    return pl.pallas_call(
        partial(branch_kernel, chunk=chunk),
        grid_spec=pltpu.PrefetchScalarGridSpec(
            num_scalar_prefetch=1,
            grid=(steps,),
            in_specs=[
                pl.BlockSpec((block, head_rows), lambda i, h: (h[0] * steps + i, 0)),
                pl.BlockSpec((width, head_rows), lambda i, h: (0, last)),
                pl.BlockSpec((block, units), lambda i, h: (h[0] * steps + i, 0)),
                pl.BlockSpec((width, units), lambda i, h: (0, 0)),
            ],
            out_specs=pl.BlockSpec((block, width), lambda i, h: (i, 0)),
        ),
        out_shape=jax.ShapeDtypeStruct((count // 2, width), BF16),
        compiler_params=params(),
        cost_estimate=cost(count * width * (units + head_rows), count * width + 2 * width * units + count * units),
        name="branch_half",
    )(half.reshape(1), heads, pack, act, down)


def weight_grad_kernel(*refs, pairs):
    out_ref = refs[-1]
    at = 0
    for pair in range(pairs):
        rows_ref, cols_ref = refs[2 * pair], refs[2 * pair + 1]
        span = slice(at, at + cols_ref.shape[1])
        out_ref[:, span] = lax.dot_general(
            rows_ref[...], cols_ref[...], (((0,), (0,)), ((), ())), preferred_element_type=F32
        ).astype(BF16)
        at += cols_ref.shape[1]


def weight_grad(pairs, count):
    width = pairs[0][0].shape[1]
    block = width // (2 * count)
    total = sum(cols.shape[1] for _, cols in pairs)
    tokens = pairs[0][0].shape[0]
    if block % LANES:
        grads = [
            jnp.einsum("rd,rc->dc", rows, cols, preferred_element_type=F32) for rows, cols in pairs
        ]
        grads = jnp.concatenate(grads, axis=1).astype(BF16).reshape(2, count, block, total)
        return grads.transpose(1, 0, 2, 3).reshape(width, total)
    specs = []
    for rows, cols in pairs:
        specs.append(pl.BlockSpec((tokens, block), lambda i: (0, (i % 2) * count + i // 2)))
        specs.append(pl.BlockSpec(cols.shape, lambda i: (0, 0)))
    return pl.pallas_call(
        partial(weight_grad_kernel, pairs=len(pairs)),
        grid=(2 * count,),
        in_specs=specs,
        out_specs=pl.BlockSpec((block, total), lambda i: (i, 0)),
        out_shape=jax.ShapeDtypeStruct((width, total), BF16),
        compiler_params=params(),
        cost_estimate=cost(2 * tokens * width * total, 2 * (tokens * (width + total) + width * total)),
        name="weight_grad",
    )(*[array for pair in pairs for array in pair])


def place_kernel(core_ref, rows_ref, *refs):
    refs[-1][...] = rows_ref[...]


def place_half(half, rows, before=None, block=256):
    count, width = rows.shape
    steps = count // block
    operands, specs = [rows], [pl.BlockSpec((block, width), lambda i, h: (i, 0))]
    if before is not None:
        operands.append(before)
        specs.append(pl.BlockSpec(memory_space=pl.ANY))
    return pl.pallas_call(
        place_kernel,
        grid_spec=pltpu.PrefetchScalarGridSpec(
            num_scalar_prefetch=1,
            grid=(steps,),
            in_specs=specs,
            out_specs=pl.BlockSpec((block, width), lambda i, h: (h[0] * steps + i, 0)),
        ),
        out_shape=jax.ShapeDtypeStruct((2 * count, width), rows.dtype),
        input_output_aliases={} if before is None else {2: 0},
        compiler_params=params(),
        cost_estimate=cost(0, 4 * count * width),
        name="place_half",
    )(half.reshape(1), *operands)


CORE = [(0, 1), (1, 0), (2, 3), (3, 2)]
YAX = [(0, 2), (2, 0), (1, 3), (3, 1)]
XAX = [(0, 1), (1, 0)]


def core_swap(block):
    return lax.ppermute(block, "tensor", CORE)


def y_swap(block):
    return lax.ppermute(block, "tensor", YAX)


def x_swap(block):
    return lax.ppermute(block, "branch", XAX)


def pick(array, index, size, axis=0):
    return lax.dynamic_slice_in_dim(array, index * size, size, axis)


def add16(first, second):
    return (first.astype(F32) + second.astype(F32)).astype(BF16)


def own_rows(array, core, why, ex):
    rows = array.shape[0]
    sixteenth = rows // 16
    first = core * 8 + why * 2 + ex
    second = core * 8 + 4 + ex * 2 + why
    return pick(array, first, sixteenth), pick(array, second, sixteenth)


def join(low_index, mine, other, axis=0):
    return jnp.where(
        low_index == 0,
        jnp.concatenate([mine, other], axis),
        jnp.concatenate([other, mine], axis),
    )


def after(value, *first):
    return lax.optimization_barrier((value,) + first)[0]


def rows_at(array, start, index, size):
    return lax.dynamic_slice_in_dim(array, start + index * size, size, 0)


def halving_send(keep, got, why, ex):
    quarter = keep.shape[0] // 2
    eighth = quarter // 2

    def send(start, index):
        return add16(rows_at(keep, start, index, eighth), rows_at(got, start, index, eighth))

    return send(0, 1 - why), send(quarter, 1 - ex)


def halving_more(keep, got, two, why, ex):
    quarter = keep.shape[0] // 2
    eighth, sixteenth = quarter // 2, quarter // 4

    def mine(start, index, received, part):
        at = start + index * eighth
        return (
            rows_at(keep, at, part, sixteenth).astype(F32)
            + rows_at(got, at, part, sixteenth).astype(F32)
            + rows_at(received, 0, part, sixteenth).astype(F32)
        )

    kept = mine(0, why, two[0], ex), mine(quarter, ex, two[1], why)
    sent = (
        mine(0, why, two[0], 1 - ex).astype(BF16),
        mine(quarter, ex, two[1], 1 - why).astype(BF16),
    )
    return kept, sent


def gather_one(first, second):
    return x_swap(first), y_swap(second)


def gather_two(first, second, got, why, ex):
    first, second = join(ex, first, got[0]), join(why, second, got[1])
    return (first, second), (y_swap(first), x_swap(second))


def gather_last(two, got, core, why, ex):
    first, second = join(why, two[0], got[0]), join(ex, two[1], got[1])
    mine = jnp.concatenate([first, second], 0)
    return mine, core_swap(mine)


def local(
    tokens,
    lengths,
    valid_mask,
    ln1_gain,
    ln1_bias,
    qkv_weight,
    qkv_bias,
    out_weight,
    out_bias,
    ln2_gain,
    ln2_bias,
    up_weight,
    up_bias,
    down_weight,
    down_bias,
    out_grad,
    *,
    count,
):
    row_count, width = tokens.shape
    ex = lax.axis_index("branch")
    tensor_at = lax.axis_index("tensor")
    why, core = tensor_at // 2, tensor_at % 2
    place = lax.axis_index("dp")
    qkv_cols = qkv_bias.shape[0] // 2
    head_rows = out_weight.shape[0] // 2
    units = up_bias.shape[0] // 2
    chunk = width // (2 * count)

    heads_shard = jnp.concatenate(
        [pick(qkv_weight, ex, qkv_cols, 1), pick(out_weight, ex, head_rows, 0).T], axis=1
    )
    up_shard = pick(up_weight, ex, units, 1)
    down_shard = pick(down_weight, ex, units, 0).T
    heads_full = lax.all_gather(heads_shard, "dp", axis=0, tiled=True)
    up_full = lax.all_gather(up_shard, "dp", axis=0, tiled=True)
    down_full = lax.all_gather(down_shard, "dp", axis=0, tiled=True)

    positions = jnp.arange(row_count, dtype=jnp.int32)
    seq_valid = (valid_mask == 1) & (positions < lengths[0])
    validity = seq_valid.astype(F32)
    key_bias = jnp.broadcast_to(
        jnp.where(seq_valid, 0.0, masked_score)[:, None], (row_count, LANES)
    )
    rows_f32 = tokens.astype(F32)
    mean = jnp.mean(rows_f32, axis=-1, keepdims=True)
    centred = rows_f32 - mean
    inv_std = lax.rsqrt(jnp.mean(centred * centred, axis=-1, keepdims=True) + norm_eps)
    unit_rows = centred * inv_std
    grad_rows = out_grad * validity.astype(BF16)[:, None]
    normed1 = (unit_rows * ln1_gain + ln1_bias).astype(BF16)
    normed2 = (unit_rows * ln2_gain + ln2_bias).astype(BF16)
    cos_table, sin_table = rope_tables(row_count, ROT)
    gap = jnp.zeros((row_count, ROT // 2), F32)
    rest = jnp.zeros((row_count, LANES - ROT), F32)
    tables = (
        jnp.concatenate([cos_table, cos_table, rest + 1.0], axis=1),
        jnp.concatenate([-sin_table, gap, rest], axis=1),
        jnp.concatenate([gap, sin_table, rest], axis=1),
    )

    qkv = project(normed1, heads_full, pick(qkv_bias, ex, qkv_cols)[None], tables)
    attended, log_total = attend(qkv, key_bias)
    attended_grad = jnp.dot(
        grad_rows, heads_full[:, qkv_cols:], preferred_element_type=F32
    ).astype(BF16)
    qkv_grad, qkv_bias_part = attend_back(
        qkv, attended_grad, log_total, key_bias, cos_table.T, sin_table.T
    )
    def scatter(partial_sum):
        return lax.psum_scatter(partial_sum, "dp", scatter_dimension=0, tiled=True)

    input_part, dot1, sum1 = dgrad_first(
        qkv_grad, heads_full, tokens, mean, inv_std, ln1_gain[None]
    )
    activated, slope = up_gelu(
        after(normed2, input_part), up_full, pick(up_bias, ex, units)[None]
    )
    down_partial = weight_grad(
        [
            (normed1, after(qkv_grad, activated)),
            (grad_rows, attended),
            (after(grad_rows, activated), activated),
        ],
        count,
    )
    first_total = scatter(down_partial)

    shift_sum = out_bias + down_bias
    tokens_own = own_rows(tokens, core, why, ex)
    validity_own = own_rows(validity, core, why, ex)
    out_grad_own = own_rows(out_grad, core, why, ex)
    mean_own = own_rows(mean, core, why, ex)
    inv_own = own_rows(inv_std, core, why, ex)

    def output_of(at, total):
        return (
            tokens_own[at].astype(F32) + validity_own[at][:, None] * (total + shift_sum)
        ).astype(BF16)

    def input_of(at, total):
        unit = (tokens_own[at].astype(F32) - mean_own[at]) * inv_own[at]
        back = inv_own[at] * (
            total
            - jnp.mean(total, axis=-1, keepdims=True)
            - unit * jnp.mean(total * unit, axis=-1, keepdims=True)
        )
        return (out_grad_own[at].astype(F32) + back).astype(BF16)

    branch_send = branch_half(
        1 - core, attended, heads_full, after(activated, down_partial), down_full
    )
    branch_core = core_swap(branch_send)
    branch_keep = branch_half(core, attended, heads_full, after(activated, branch_send), down_full)
    branch_core = after(branch_core, branch_keep)
    branch_two = halving_send(branch_keep, branch_core, why, ex)
    branch_two_got = y_swap(branch_two[0]), x_swap(branch_two[1])
    hidden_grad, up_bias_part = hidden_back(
        after(grad_rows, branch_keep, *branch_two), down_full, slope
    )
    norm_rows = tokens, mean, inv_std, ln2_gain[None], input_part
    branch_two_got = after(branch_two_got, hidden_grad)
    branch_mine, branch_three = halving_more(branch_keep, branch_core, branch_two_got, why, ex)
    branch_three_got = x_swap(branch_three[0]), y_swap(branch_three[1])
    input_send, dot2, sum2 = dgrad_half(
        1 - core, after(hidden_grad, *branch_three), up_full, *norm_rows
    )
    input_core = core_swap(input_send)
    input_keep, dot3, sum3 = dgrad_half(core, after(hidden_grad, input_send), up_full, *norm_rows)
    input_core = after(input_core, input_keep)
    input_two = halving_send(input_keep, input_core, why, ex)
    input_two_got = y_swap(input_two[0]), x_swap(input_two[1])
    branch_three_got = after(branch_three_got, *input_two)
    output_one = [
        output_of(at, branch_mine[at] + branch_three_got[at].astype(F32)) for at in range(2)
    ]
    output_got = gather_one(*output_one)
    dot2, sum2 = dot2 + dot3, sum2 + sum3
    vectors = jnp.concatenate(
        [
            dot1[0],
            sum1[0],
            dot2[0],
            sum2[0],
            jnp.sum(grad_rows, axis=0, dtype=F32),
            qkv_bias_part[0],
            up_bias_part[0],
        ]
    ).reshape(-1, LANES)
    hops = [
        lax.ppermute(vectors, "dp", [(k, (k + hop) % count) for k in range(count)])
        for hop in range(1, count)
    ]
    up_partial = weight_grad([(after(normed2, vectors, *output_one), hidden_grad)], count)
    up_total = scatter(up_partial)
    input_two_got = after(input_two_got, up_partial)
    input_mine, input_three = halving_more(input_keep, input_core, input_two_got, why, ex)
    input_three_got = x_swap(input_three[0]), y_swap(input_three[1])
    output_got, hops = after((output_got, hops), *input_three)
    output_two, output_got = gather_two(*output_one, output_got, why, ex)
    vectors = sum(after(hops, *output_two), vectors)
    norm_count, bias_rows = 4 * width // LANES, width // LANES
    norms, bias_grad, biases = (
        vectors[:norm_count],
        vectors[norm_count : norm_count + bias_rows].reshape(width),
        vectors[norm_count + bias_rows :],
    )
    norms_other, biases_other = core_swap(norms), x_swap(biases)
    input_three_got = after(input_three_got, norms, *output_two)
    input_one = [input_of(at, input_mine[at] + input_three_got[at].astype(F32)) for at in range(2)]
    input_got = gather_one(*input_one)
    norms, biases_other = after((norms + norms_other, biases_other), *input_one)
    norms_other = y_swap(norms)
    output_got = after(output_got, norms, *input_one)
    output_mine, output_other = gather_last(output_two, output_got, core, why, ex)
    input_got, norms_other = after((input_got, norms_other), output_mine)
    norms = norms + norms_other
    norms_other = x_swap(norms)
    input_got = after(input_got, norms)
    input_two, input_got = gather_two(*input_one, input_got, why, ex)
    def halves(total):
        return pick(total, ex, chunk).astype(F32), pick(total, 1 - ex, chunk)

    first_mine, first_given = halves(after(first_total, *input_two))
    first_other = x_swap(first_given)
    output_half = place_half(core, after(output_mine, first_given, *input_two))
    output_rows = place_half(1 - core, after(output_other, output_half), output_half)
    biases, other = biases.reshape(-1), biases_other.reshape(-1)
    qkv_bias_grad = join(ex, biases[:qkv_cols], other[:qkv_cols])
    up_bias_grad = join(ex, biases[qkv_cols:], other[qkv_cols:])
    input_got, norms_other = after((input_got, norms_other), output_rows)
    norms = (norms + norms_other).reshape(4, width)
    input_mine, input_other = gather_last(input_two, input_got, core, why, ex)
    grad_half = place_half(core, after(input_mine, norms))
    up_mine, up_given = halves(after(up_total, grad_half))
    up_other = x_swap(up_given)
    grad_input = place_half(1 - core, after(input_other, up_given), grad_half)
    first_other = after(first_other, grad_input)
    heads_mine, down_mine = first_mine[:, :-units], first_mine[:, -units:]
    other, down_other = first_other[:, :-units].astype(F32), first_other[:, -units:].astype(F32)
    qkv_out = join(ex, heads_mine[:, :qkv_cols], other[:, :qkv_cols], 1)
    out_out = join(ex, heads_mine[:, qkv_cols:].T, other[:, qkv_cols:].T, 0)
    down_out = join(ex, down_mine.T, down_other.T, 0)
    up_other = after(up_other, qkv_out, out_out, down_out, grad_input)
    up_out = join(ex, up_mine, up_other.astype(F32), 1)

    return (
        output_rows,
        grad_input,
        norms[0],
        norms[1],
        qkv_out,
        qkv_bias_grad,
        out_out,
        bias_grad,
        norms[2],
        norms[3],
        up_out,
        up_bias_grad,
        down_out,
        bias_grad,
    )


def solution(mesh):
    return jax.shard_map(
        partial(local, count=mesh.shape["dp"]),
        mesh=mesh,
        in_specs=(
            P("dp", None),
            P("dp"),
            P("dp"),
            P(),
            P(),
            P("dp", "tensor"),
            P("tensor"),
            P("tensor", "dp"),
            P(),
            P(),
            P(),
            P("dp", "tensor"),
            P("tensor"),
            P("tensor", "dp"),
            P(),
            P("dp", None),
        ),
        out_specs=(
            P("dp", None),
            P("dp", None),
            P(),
            P(),
            P(("branch", "dp"), "tensor"),
            P("tensor"),
            P("tensor", ("branch", "dp")),
            P(),
            P(),
            P(),
            P(("branch", "dp"), "tensor"),
            P("tensor"),
            P("tensor", ("branch", "dp")),
            P(),
        ),
        check_vma=False,
    )
```
